256 devices in a mesh: blocks: 64 (over x, z, core), rep: 4 (over y).
Axes of the slice: x: 4, y: 4, z: 8, core: 2. Of those that a mesh axis runs over, the one named last changes fastest.
Arguments:
- features: bfloat16 [4, 256, 512, 128], P('rep', 'blocks'), may hold values from -6 to 6
- weight_one: bfloat16 [27, 128, 128], replicated, may hold values from -0.109375 to 0.109375
- weight_two: bfloat16 [27, 128, 128], replicated, may hold values from -0.109375 to 0.109375
- cotangent: bfloat16 [4, 256, 512, 128], P('rep', 'blocks'), may hold values from -6 to 6
- neighbours: int32 [4, 256, 26], P('rep', 'blocks'), may hold values from -1 to 255, as said below
Outputs:
- segment_out: bfloat16 [4, 256, 512, 128], P('rep', 'blocks')
- grad_one: float32 [27, 128, 128], replicated
- grad_two: float32 [27, 128, 128], replicated
The draws below stay inside these ranges and needn't reach their ends.
Inputs may be any that keep to these rules, and one draw needn't show every extreme that they name: neighbours[s, b, k] is the active block at offset k from block b in the slab of scene s, or -1 where that block is empty or outside the slab; blocks are ordered by x, then within each cross-section of 4 x 4 blocks by the Morton alternate of y and z, taken in reverse on odd x; block b belongs to device b // 4 of the axis blocks; the relation is symmetric (b names n at an offset exactly when n names b at the opposite one); the devices of a block and of any of its neighbours differ by at most 7 in index, and in every scene some pair differs by exactly 7.
All inputs are finite; a program needn't handle non-finite values.
Results may differ from the reference program's by a relative error of at most 0.005.
Values may be sent and summed in bfloat16 or wider, within the bound.
No kernel may reach another device: no remote copies, remote signals or barrier semaphores. Data moves between devices by JAX's collectives and lax.ppermute only.
A program may use at most 128 MiB of HBM per device.

```python
import math
import jax
import jax.numpy as jnp
import numpy as np
from jax import lax

CH = 128
BLOCKS_DEV = 4
TOTAL_BLOCKS = 256
SCENES = 4


def offset_list_drawn():
    return [(step_x, step_y, step_z) for step_x in (-1, 0, 1) for step_y in (-1, 0, 1) for step_z in (-1, 0, 1) if (step_x, step_y, step_z) != (0, 0, 0)]


def morton_code(coord_y, coord_z):
    return coord_y % 2 + 2 * (coord_z % 2) + 4 * (coord_y // 2) + 8 * (coord_z // 2)


def morton_y(morton_val):
    return morton_val % 2 + 2 * (morton_val // 4 % 2)


def morton_z(morton_val):
    return morton_val // 2 % 2 + 2 * (morton_val // 8 % 2)


def slice_cells(perm_key, slice_count, forced):
    if forced:
        perm_part = jax.random.permutation(perm_key, 15).astype(jnp.int32)
        inverse_part = jnp.zeros((15,), jnp.int32).at[perm_part].set(jnp.arange(15, dtype=jnp.int32))
        return jnp.concatenate([(inverse_part < slice_count - 1).astype(jnp.int32), jnp.ones((1,), jnp.int32)])
    perm_all = jax.random.permutation(perm_key, 16).astype(jnp.int32)
    inverse_all = jnp.zeros((16,), jnp.int32).at[perm_all].set(jnp.arange(16, dtype=jnp.int32))
    return (inverse_all < slice_count).astype(jnp.int32)


def scene_links(scene_key):
    reach_val = (BLOCKS_DEV + 24) // BLOCKS_DEV
    lead_count = max(0, reach_val * BLOCKS_DEV - 31)
    slice_total = TOTAL_BLOCKS // 10 + 3
    span_cap = (reach_val + 1) * BLOCKS_DEV
    cell_total = 16 * slice_total
    first_order = jnp.zeros((), jnp.int32)
    last_first = jnp.zeros((), jnp.int32)
    last_count = jnp.zeros((), jnp.int32)
    by_position = []
    for slice_id in range(slice_total):
        hole_key, perm_key = jax.random.split(jax.random.fold_in(scene_key, slice_id + 1))
        wanted = (16 - jax.random.randint(hole_key, (), 0, 3)).astype(jnp.int32)
        if slice_id == 0:
            slice_count = jnp.full((), lead_count, jnp.int32)
        elif slice_id == 1:
            slice_count = jnp.full((), 16, jnp.int32)
        else:
            slice_count = jnp.minimum(wanted, span_cap - last_first % BLOCKS_DEV - last_count)
            if slice_id == 2:
                slice_count = jnp.maximum(slice_count, reach_val * BLOCKS_DEV - 15 - lead_count)
        slice_count = slice_count.astype(jnp.int32)
        occupied_m = slice_cells(perm_key, slice_count, slice_id in (1, 2))
        by_position.append(occupied_m if slice_id % 2 == 0 else occupied_m[::-1])
        last_first = first_order
        last_count = slice_count
        first_order = (first_order + slice_count).astype(jnp.int32)
    occupied = jnp.concatenate(by_position).astype(jnp.int32)
    order_pos = (jnp.cumsum(occupied) - 1).astype(jnp.int32)
    active = (occupied == 1) & (order_pos < TOTAL_BLOCKS)
    cell_codes = jnp.arange(cell_total, dtype=jnp.int32)
    block_codes = jnp.zeros((TOTAL_BLOCKS,), jnp.int32).at[jnp.where(active, order_pos, TOTAL_BLOCKS)].set(cell_codes, mode='drop')
    coord_x = block_codes // 16
    place_in = block_codes % 16
    morton_val = jnp.where(coord_x % 2 == 0, place_in, 15 - place_in)
    coord_y = morton_y(morton_val)
    coord_z = morton_z(morton_val)
    columns = []
    for offset in offset_list_drawn():
        near_x = coord_x + offset[0]
        near_y = coord_y + offset[1]
        near_z = coord_z + offset[2]
        inside = (near_x >= 0) & (near_x < slice_total) & (near_y >= 0) & (near_y <= 3) & (near_z >= 0) & (near_z <= 3)
        safe_x = jnp.clip(near_x, 0, slice_total - 1)
        safe_m = morton_code(jnp.clip(near_y, 0, 3), jnp.clip(near_z, 0, 3))
        near_code = (16 * safe_x + jnp.where(safe_x % 2 == 0, safe_m, 15 - safe_m)).astype(jnp.int32)
        inside = inside & active[near_code]
        columns.append(jnp.where(inside, order_pos[near_code], -1))
    return jnp.stack(columns, axis=1).astype(jnp.int32)


def draw_neighbours(key, part):
    scene_keys = jax.random.split(key, SCENES)
    return jax.vmap(scene_links)(scene_keys)


def steps_of(key, shape, cuts, least, top_value):
    factor_of = 1.0
    for dim, shards_of in cuts:
        draws = jax.random.uniform(jax.random.fold_in(jax.random.fold_in(key, 6), dim), (shards_of,), jnp.float32, least / len(cuts), top_value / len(cuts))
        factor_of = factor_of * jnp.repeat(jnp.exp(draws), shape[dim] // shards_of).reshape((-1,) + (1,) * (len(shape) - 1 - dim))
    return factor_of


def noise(rng, dims, width, bound, cuts=(), kind=jnp.bfloat16):
    result = width * jax.random.normal(rng, dims, jnp.float32)
    if cuts:
        result = result * steps_of(rng, dims, cuts, -0.22, 0.18)
    return jnp.clip(result, -bound, bound).astype(kind)


def setup_inputs(seed: int = 0) -> dict:
    keys = jax.random.split(jax.random.key(seed), 6)
    return {
        "features": noise(keys[0], (SCENES, TOTAL_BLOCKS, 512, CH), 1.0, 6.0, ((0, 4), (1, 64))),
        "weight_one": noise(keys[1], (27, CH, CH), (27 * CH) ** -0.5, 0.109375),
        "weight_two": noise(keys[2], (27, CH, CH), (27 * CH) ** -0.5, 0.109375),
        "cotangent": noise(keys[3], (SCENES, TOTAL_BLOCKS, 512, CH), 1.0, 6.0, ((0, 4), (1, 64))),
        "neighbours": draw_neighbours(jax.random.fold_in(keys[5], 71), 0),
    }


def offset_list():
    return [(step_x, step_y, step_z) for step_x in (-1, 0, 1) for step_y in (-1, 0, 1) for step_z in (-1, 0, 1) if (step_x, step_y, step_z) != (0, 0, 0)]

def source_range(step_val):
    if step_val == 1:
        return (0, 1)
    if step_val == -1:
        return (7, 8)
    return (0, 8)

def voxel_index(offset):
    ranges = [source_range(step_val) for step_val in offset]
    along_i = np.arange(ranges[0][0], ranges[0][1])
    along_j = np.arange(ranges[1][0], ranges[1][1])
    along_l = np.arange(ranges[2][0], ranges[2][1])
    flat_index = (along_i[:, None, None] * 64 + along_j[None, :, None] * 8 + along_l[None, None, :]).reshape(-1)
    sub_shape = (len(along_i), len(along_j), len(along_l))
    return (flat_index, sub_shape)

def build_padded(own_blocks, table, placed):
    block_count = own_blocks.shape[0]
    channels = own_blocks.shape[2]
    pieces = {(0, 0, 0): own_blocks.reshape(block_count, 8, 8, 8, channels)}
    for k_index, offset in enumerate(offset_list()):
        flat_index, sub_shape = voxel_index(offset)
        picked = jnp.take(table, jnp.asarray(flat_index, dtype=jnp.int32), axis=1)
        column = placed[:, k_index]
        got_rows = jnp.take(picked, jnp.maximum(column, 0).astype(jnp.int32), axis=0)
        got_rows = jnp.where((column >= 0)[:, None, None], got_rows, jnp.zeros_like(got_rows))
        pieces[offset] = got_rows.reshape((block_count,) + sub_shape + (channels,))
    planes = []
    for step_x in (-1, 0, 1):
        lines = []
        for step_y in (-1, 0, 1):
            lines.append(jnp.concatenate([pieces[step_x, step_y, step_z] for step_z in (-1, 0, 1)], axis=3))
        planes.append(jnp.concatenate(lines, axis=2))
    return jnp.concatenate(planes, axis=1)

def tap_slab(padded, tap_a):
    block_count = padded.shape[0]
    channels = padded.shape[-1]
    return jnp.concatenate([padded[:, tap_a:tap_a + 8, tap_b:tap_b + 8, tap_c:tap_c + 8, :].reshape(block_count * 512, channels) for tap_b in range(3) for tap_c in range(3)], axis=1)

def conv_taps(padded, weights):
    block_count = padded.shape[0]
    channels = padded.shape[-1]
    summed = jnp.zeros((block_count * 512, weights.shape[2]), jnp.float32)
    for tap_a in range(3):
        kernel = weights[9 * tap_a:9 * tap_a + 9].reshape(9 * channels, weights.shape[2])
        summed = summed + jnp.dot(tap_slab(padded, tap_a), kernel, preferred_element_type=jnp.float32)
    return summed

def weight_taps(padded, grad_rows):
    channels = padded.shape[-1]
    width_out = grad_rows.shape[1]
    parts_list = []
    for tap_a in range(3):
        product = lax.dot_general(tap_slab(padded, tap_a), grad_rows, (((0,), (0,)), ((), ())), preferred_element_type=jnp.float32)
        parts_list.append(product.reshape(9, channels, width_out))
    return jnp.concatenate(parts_list, axis=0)

def silu_slope(values):
    sigmoid_val = jax.nn.sigmoid(values)
    return sigmoid_val * (1.0 + values * (1.0 - sigmoid_val))

def reference(features, weight_one, weight_two, cotangent, neighbours):
    flipped = jnp.transpose(weight_two[::-1], (0, 2, 1))
    grad_one = jnp.zeros((27, CH, CH), jnp.float32)
    grad_two = jnp.zeros((27, CH, CH), jnp.float32)
    outputs = []
    for scene_index in range(SCENES):
        blocks = features[scene_index]
        cot_blocks = cotangent[scene_index]
        link_table = neighbours[scene_index]
        input_pad = build_padded(blocks, blocks, link_table)
        pre_act = conv_taps(input_pad, weight_one)
        hidden = jax.nn.silu(pre_act).astype(jnp.bfloat16)
        hidden_blocks = hidden.reshape(TOTAL_BLOCKS, 512, CH)
        hidden_pad = build_padded(hidden_blocks, hidden_blocks, link_table)
        outputs.append(conv_taps(hidden_pad, weight_two).astype(jnp.bfloat16).reshape(TOTAL_BLOCKS, 512, CH))
        grad_two = grad_two + weight_taps(hidden_pad, cot_blocks.reshape(-1, CH))
        cot_pad = build_padded(cot_blocks, cot_blocks, link_table)
        back_rows = conv_taps(cot_pad, flipped)
        delta_rows = (back_rows * silu_slope(pre_act)).astype(jnp.bfloat16)
        grad_one = grad_one + weight_taps(input_pad, delta_rows)
    norm_scale = 1.0 / math.sqrt(SCENES * TOTAL_BLOCKS * 512)
    return (jnp.stack(outputs), grad_one * norm_scale, grad_two * norm_scale)
```

```python
import functools
import math

import jax
import jax.numpy as jnp
from jax import lax
from jax.experimental import pallas as pl
from jax.experimental.pallas import tpu as pltpu
from jax.sharding import PartitionSpec as P


CH = 128
BD = 4
RX, RE, RP = 256, 128, 256
FULL, MID, FAR = RX + RE + 2 * RP, RX + RE, RX
SLOTS = 20

OFFSETS = [
    (dx, dy, dz)
    for dx in (-1, 0, 1)
    for dy in (-1, 0, 1)
    for dz in (-1, 0, 1)
    if (dx, dy, dz) != (0, 0, 0)
]
K_OF = {offset: k for k, offset in enumerate(OFFSETS)}
BF = jnp.bfloat16
F32 = jnp.float32


def pack_field(nb, dev, own, down, up, fields, f):
    ox, oe = f * RX, fields * RX + f * RE
    oj = fields * (RX + RE) + f * RP
    ol = fields * (RX + RE + RP) + f * RP

    def body(b, carry):
        me = dev * BD + b

        def neighbour(offset):
            return nb[b, K_OF[offset]]

        y_hi, y_lo = neighbour((0, 1, 0)), neighbour((0, -1, 0))
        z_hi, z_lo = neighbour((0, 0, 1)), neighbour((0, 0, -1))
        cases = (
            (down, 0, (y_hi >= 0) & (y_hi < me), (z_hi >= 0) & (z_hi < me)),
            (up, 448, jnp.logical_not(y_lo > me), jnp.logical_not(z_lo > me)),
        )
        edges = jnp.concatenate(
            [own[b, pl.ds(js * 8 + ls, 8, stride=64), :] for js in (0, 7) for ls in (0, 7)], axis=0
        ).astype(BF)
        z_low = own[b, pl.ds(0, 64, stride=8), :]
        z_high = own[b, pl.ds(7, 64, stride=8), :]
        y_low = jnp.concatenate([own[b, i * 64 : i * 64 + 8, :] for i in range(8)], axis=0)
        y_high = jnp.concatenate([own[b, i * 64 + 56 : i * 64 + 64, :] for i in range(8)], axis=0)
        for ref, x_row, take_y, take_z in cases:
            ref[pl.ds(pl.multiple_of(ox + b * 64, 64), 64), :] = own[b, x_row : x_row + 64, :].astype(BF)
            ref[pl.ds(pl.multiple_of(oe + b * 32, 32), 32), :] = edges
            ref[pl.ds(pl.multiple_of(oj + b * 64, 64), 64), :] = jnp.where(take_y, y_high, y_low).astype(BF)
            ref[pl.ds(pl.multiple_of(ol + b * 64, 64), 64), :] = jnp.where(take_z, z_high, z_low).astype(BF)
        return carry

    lax.fori_loop(0, BD, body, 0)


def fill_tables(core, pieces, tx, te, tj, tl, fields, f):
    own_down, own_up, d1, u1, d2, u2, d3, u3, swapped = pieces
    full, mid, far = fields * FULL, fields * MID, fields * FAR
    turn = 2 * core
    at = 0
    plan = [
        (own_down, 0, 10, 4),
        (own_up, 0, 9, 4),
        (d1, 0, 12, 4),
        (u1, 0, 7, 4),
        (d2, 0, 14, 2),
        (u2, 0, 5, 2),
        (d3, 0, 16, 1),
        (u3, 0, 3, 1),
    ]
    for slot, kind, size in (
        (11 - 3 * core, 4, full),
        (13 - turn, 4, full),
        (8 - turn, 4, full),
        (15 - turn, 2, mid),
        (6 - turn, 2, mid),
        (17 - turn, 1, far),
        (4 - turn, 1, far),
        (2 + 15 * core, 1, far),
    ):
        plan.append((swapped, at, slot, kind))
        at += size
    for ref, base, slot, kind in plan:
        row = base + f * RX
        tx[slot] = ref[row : row + RX, :].astype(F32).reshape(BD, 64, CH)
        if kind >= 2:
            row = base + fields * RX + f * RE
            te[slot] = ref[row : row + RE, :].astype(F32).reshape(BD, 32, CH)
        if kind >= 4:
            row = base + fields * (RX + RE) + f * RP
            tj[slot] = ref[row : row + RP, :].astype(F32).reshape(BD, 64, CH)
            row += fields * RP
            tl[slot] = ref[row : row + RP, :].astype(F32).reshape(BD, 64, CH)


def build_shifted(nb, dev, own, tx, te, tj, tl, cf, lf, rf, sh):
    def block(b, carry):
        me = dev * BD + b

        def source(offset):
            n = nb[b, K_OF[offset]]
            gap = lax.shift_right_logical(jnp.maximum(n, 0), 2) - dev
            slot = jnp.clip(jnp.where(n > me, 10 + gap, 9 + gap), 0, SLOTS - 1)
            return n >= 0, slot, jnp.maximum(n, 0) & 3

        def keep(valid, rows):
            return jnp.where(valid, rows, jnp.zeros_like(rows))

        for i in range(8):
            cf[b, pl.ds((i + 1) * 80 + 8, 64), :] = own[b, pl.ds(i * 64, 64), :]
        for dy, line in ((-1, 0), (1, 9)):
            valid, slot, loc = source((0, dy, 0))
            for i in range(8):
                rows = tj[slot, loc, pl.ds(i * 8, 8), :]
                cf[b, pl.ds((i + 1) * 80 + line * 8, 8), :] = keep(valid, rows)
        for dx, plane in ((-1, 0), (1, 9)):
            valid, slot, loc = source((dx, 0, 0))
            cf[b, pl.ds(plane * 80 + 8, 64), :] = keep(valid, tx[slot, loc])
            for dy, line, j in ((-1, 0, 7), (1, 9, 0)):
                valid, slot, loc = source((dx, dy, 0))
                rows = tx[slot, loc, pl.ds(j * 8, 8), :]
                cf[b, pl.ds(plane * 80 + line * 8, 8), :] = keep(valid, rows)
        for plane in range(10):
            lines = cf[b, pl.ds(plane * 80, 80), :].reshape(10, 8, CH)
            lf[b, pl.ds(plane * 80, 80), :] = pltpu.roll(lines, 1, 1).reshape(80, CH)
            rf[b, pl.ds(plane * 80, 80), :] = pltpu.roll(lines, 7, 1).reshape(80, CH)
        for dz, ref, cell, l in ((-1, lf, 0, 7), (1, rf, 7, 0)):
            valid, slot, loc = source((0, 0, dz))
            for i in range(8):
                rows = tl[slot, loc, pl.ds(i * 8, 8), :]
                ref[b, pl.ds((i + 1) * 80 + 8 + cell, 8, stride=8), :] = keep(valid, rows)
            for dy, line, j in ((-1, 0, 7), (1, 9, 0)):
                valid, slot, loc = source((0, dy, dz))
                edge = (2 * (j // 7) + l // 7) * 8
                rows = te[slot, loc, pl.ds(edge, 8), :]
                ref[b, pl.ds(80 + line * 8 + cell, 8, stride=80), :] = keep(valid, rows)
            for dx, plane in ((-1, 0), (1, 9)):
                valid, slot, loc = source((dx, 0, dz))
                rows = tx[slot, loc, pl.ds(l, 8, stride=8), :]
                ref[b, pl.ds(plane * 80 + 8 + cell, 8, stride=8), :] = keep(valid, rows)
                for dy, line, j in ((-1, 0, 7), (1, 9, 0)):
                    valid, slot, loc = source((dx, dy, dz))
                    rows = tx[slot, loc, pl.ds(j * 8 + l, 1), :]
                    ref[b, pl.ds(plane * 80 + line * 8 + cell, 1), :] = keep(valid, rows)
        return carry

    lax.fori_loop(0, BD, block, 0)

    def join(plane, carry):
        row = pl.multiple_of(plane * 80, 80)
        for pair in range(2):
            for c, ref in ((0, lf), (1, cf), (2, rf)):
                halves = [ref[2 * pair + h, pl.ds(row, 80), :].reshape(10, 8, CH) for h in (0, 1)]
                sh[c, pair, plane] = jnp.concatenate(halves, axis=1).astype(BF)
        return carry

    lax.fori_loop(0, 10, join, 0)


def slabs(sh, pair, first, count, taps):
    return jnp.concatenate(
        [
            sh[c, pair, pl.ds(first + a, count), b : b + 8].reshape(count * 128, CH)
            for a, b, c in taps
        ],
        axis=1,
    )


TAPS = [(a, b, c) for a in range(3) for b in range(3) for c in range(3)]
CHUNK = 4


def conv(sh, weight, emit):
    def body(step, carry):
        pair = step // (8 // CHUNK)
        first = (step % (8 // CHUNK)) * CHUNK
        rows = jnp.dot(slabs(sh, pair, first, CHUNK, TAPS), weight[...], preferred_element_type=F32)
        emit(pair, first, rows)
        return carry

    lax.fori_loop(0, 2 * (8 // CHUNK), body, 0)


def split_blocks(pair, first, rows, store):
    lines = rows.reshape(CHUNK * 8, 16, CH)
    for h in (0, 1):
        part = lines[:, 8 * h : 8 * h + 8].reshape(CHUNK * 64, CH)
        store(2 * pair + h, pl.multiple_of(first * 64, 64), part)


def load_own(ref, own):
    for b in range(BD):
        own[b] = ref[b].astype(F32)


def pack_kernel(nb, dev, feat, cot, down, up, own):
    for f, ref in enumerate((feat, cot)):
        load_own(ref, own)
        pack_field(nb, dev[0], own, down, up, 2, f)


def forward_kernel(nb, dev, feat, *refs):
    pieces, weight = refs[:9], refs[9]
    hid, hid_s, pre, down, up, sh, own, tx, te, tj, tl, cf, lf, rf = refs[10:]
    load_own(feat, own)
    fill_tables(dev[0] & 1, pieces, tx, te, tj, tl, 2, 0)
    build_shifted(nb, dev[0], own, tx, te, tj, tl, cf, lf, rf, sh)

    def emit(pair, first, rows):
        at = pl.ds(pl.multiple_of(pair * 1024 + first * 128, 128), CHUNK * 128)
        pre[at, :] = rows
        act = (rows / (1.0 + jnp.exp(-rows))).astype(BF)
        hid_s[at, :] = act

        def store(b, row, part):
            own[b, pl.ds(row, CHUNK * 64), :] = part
            hid[b, pl.ds(row, CHUNK * 64), :] = part.astype(BF)

        split_blocks(pair, first, act.astype(F32), store)

    conv(sh, weight, emit)
    pack_field(nb, dev[0], own, down, up, 1, 0)


def backward_kernel(nb, dev, cot, *refs):
    pieces, weight, hid_s, pre, sh_feat = refs[:9], refs[9], refs[10], refs[11], refs[12]
    grads, sh, own, tx, te, tj, tl, cf, lf, rf, delta, hid_t, delta_t, acc = refs[13:]
    load_own(cot, own)
    fill_tables(dev[0] & 1, pieces, tx, te, tj, tl, 2, 1)
    build_shifted(nb, dev[0], own, tx, te, tj, tl, cf, lf, rf, sh)

    def emit(pair, first, rows):
        at = pl.ds(pl.multiple_of(pair * 1024 + first * 128, 128), CHUNK * 128)
        v = pre[at, :]
        sig = 1.0 / (1.0 + jnp.exp(-v))
        delta[at, :] = (rows * (sig * (1.0 + v * (1.0 - sig)))).astype(BF)

    conv(sh, weight, emit)
    for pair in range(2):
        hid_t[pair] = hid_s[pair * 1024 : pair * 1024 + 1024, :].T
        delta_t[pair] = delta[pair * 1024 : pair * 1024 + 1024, :].T

    def product(left, right, a, b):
        taps = [(a, b, c) for c in range(3)]
        total = jnp.dot(left[0], slabs(right, 0, 0, 8, taps), preferred_element_type=F32)
        return total + jnp.dot(left[1], slabs(right, 1, 0, 8, taps), preferred_element_type=F32)

    def body(step, carry):
        a, b = step // 3, step % 3
        taps = [(a, b, c) for c in range(3)]

        def cut(ref, pair):
            return jnp.concatenate(
                [ref[c, pair, pl.ds(a, 8), pl.ds(b, 8)].reshape(1024, CH) for c in range(3)], axis=1
            )

        one = jnp.dot(delta_t[0], cut(sh_feat, 0), preferred_element_type=F32)
        one = one + jnp.dot(delta_t[1], cut(sh_feat, 1), preferred_element_type=F32)
        two = jnp.dot(hid_t[0], cut(sh, 0), preferred_element_type=F32)
        two = two + jnp.dot(hid_t[1], cut(sh, 1), preferred_element_type=F32)
        for c in range(3):
            row = pl.multiple_of((step * 3 + c) * CH, CH)
            grads[pl.ds(row, CH), :] = one[:, c * CH : c * CH + CH].T
            row = pl.multiple_of((53 - step * 3 - c) * CH, CH)
            grads[pl.ds(row, CH), :] = two[:, c * CH : c * CH + CH]
        return carry

    lax.fori_loop(0, 9, body, 0)


def second_kernel(nb, dev, hid, *refs):
    pieces, weight, out = refs[:9], refs[9], refs[10]
    own, tx, te, tj, tl, cf, lf, rf, sh = refs[11:]
    load_own(hid, own)
    fill_tables(dev[0] & 1, pieces, tx, te, tj, tl, 1, 0)
    build_shifted(nb, dev[0], own, tx, te, tj, tl, cf, lf, rf, sh)

    def emit(pair, first, rows):
        def store(b, row, part):
            out[b, pl.ds(row, CHUNK * 64), :] = part.astype(BF)

        split_blocks(pair, first, rows, store)

    conv(sh, weight, emit)


def scratch_own():
    return [pltpu.VMEM((BD, 512, CH), F32)]


def scratch_build():
    return [
        pltpu.VMEM((SLOTS, BD, 64, CH), F32),
        pltpu.VMEM((SLOTS, BD, 32, CH), F32),
        pltpu.VMEM((SLOTS, BD, 64, CH), F32),
        pltpu.VMEM((SLOTS, BD, 64, CH), F32),
    ] + [pltpu.VMEM((BD, 800, CH), F32)] * 3


SHIFTED = (3, 2, 10, 10, 16, CH)


def call(kernel, outs, scratch, nb, dev, *arrays):
    smem = pl.BlockSpec(memory_space=pltpu.SMEM)
    vmem = pl.BlockSpec(memory_space=pltpu.VMEM)
    return pl.pallas_call(
        kernel,
        out_shape=[jax.ShapeDtypeStruct(shape, dtype) for shape, dtype in outs],
        in_specs=[smem, smem] + [vmem] * len(arrays),
        out_specs=[vmem] * len(outs),
        scratch_shapes=scratch,
    )(nb, dev, *arrays)


def exchange(down, up, fields, core, chips_z):
    size = lax.axis_size("blocks")

    def to(x, shift):
        return lax.ppermute(x, "blocks", [(i, (i + shift) % size) for i in range(size)])

    full, mid, far = fields * FULL, fields * MID, fields * FAR
    d1, u1 = to(down, -2), to(up, 2)
    d2, u2 = to(d1[:mid], -2), to(u1[:mid], 2)
    d3, u3 = to(d2[:far], -2), to(u2[:far], 2)
    last = jnp.where(core == 0, d3, u3)
    v4 = lax.ppermute(
        last, "blocks", [(i, (i - 2 if i % 2 == 0 else i + 2) % size) for i in range(size)]
    )
    mine = jnp.where(core == 0, up, down)
    parcel = jnp.concatenate([mine, d1, u1, d2, u2, d3, u3, v4], axis=0)
    swapped = lax.ppermute(parcel, "blocks", [(i, i ^ 1) for i in range(size)])
    return (down, up, d1, u1, d2, u2, d3, u3, swapped)


def reduce_all(grads, core, scale):
    size, reps = lax.axis_size("blocks"), lax.axis_size("rep")
    half = grads.shape[0] // 2
    chips = size // 2
    pairs = [(i, i ^ 1) for i in range(size)]
    groups = [[c + 2 * k for k in range(chips)] for c in range(2)]
    one, two = grads[:half], grads[half:]
    theirs = lax.ppermute(jnp.where(core == 0, two, one), "blocks", pairs)
    mine = jnp.where(core == 0, one, two) + theirs
    part = mine.astype(BF).reshape(reps, half // reps, CH)
    part = lax.all_to_all(part, "rep", 0, 0, tiled=True)
    part = jnp.sum(part.astype(F32), axis=0)
    rows = half // reps // chips
    part = part.reshape(chips, rows, CH)
    part = lax.all_to_all(part, "blocks", 0, 0, axis_index_groups=groups, tiled=True)
    part = (jnp.sum(part, axis=0) * scale).astype(BF)
    part = jnp.broadcast_to(part[None], (chips, rows, CH))
    part = lax.all_to_all(part, "blocks", 0, 0, axis_index_groups=groups, tiled=True)
    mine = lax.all_gather(part.reshape(half // reps, CH), "rep", tiled=True)
    theirs = lax.ppermute(mine, "blocks", pairs)
    shape = (half // CH, CH, CH)
    one = jnp.where(core == 0, mine, theirs).astype(F32).reshape(shape)
    two = jnp.where(core == 0, theirs, mine).astype(F32).reshape(shape)
    return one, two


def local(features, weight_one, weight_two, cotangent, neighbours):
    feat, cot, nb = features[0], cotangent[0], neighbours[0]
    index = lax.axis_index("blocks")
    core = index % 2
    dev = index.astype(jnp.int32).reshape(1)
    w_one = weight_one.reshape(27 * CH, CH)
    w_two = weight_two.reshape(27 * CH, CH)
    flipped = jnp.transpose(weight_two[::-1], (0, 2, 1)).reshape(27 * CH, CH)
    two_fields = (2 * FULL, CH)
    down, up = call(pack_kernel, [(two_fields, BF)] * 2, scratch_own(), nb, dev, feat, cot)
    pieces = exchange(down, up, 2, core, 8)
    hid, hid_s, pre, hid_down, hid_up, sh_feat = call(
        forward_kernel,
        [
            ((BD, 512, CH), BF),
            ((BD * 512, CH), BF),
            ((BD * 512, CH), F32),
            ((FULL, CH), BF),
            ((FULL, CH), BF),
            (SHIFTED, BF),
        ],
        scratch_own() + scratch_build(),
        nb,
        dev,
        feat,
        *pieces,
        w_one,
    )
    hid_pieces = exchange(hid_down, hid_up, 1, core, 8)
    (grads,) = call(
        backward_kernel,
        [((54 * CH, CH), F32)],
        [pltpu.VMEM(SHIFTED, BF)]
        + scratch_own()
        + scratch_build()
        + [
            pltpu.VMEM((BD * 512, CH), BF),
            pltpu.VMEM((2, CH, 1024), BF),
            pltpu.VMEM((2, CH, 1024), BF),
            pltpu.VMEM((8, CH), F32),
        ],
        nb,
        dev,
        cot,
        *pieces,
        flipped,
        hid_s,
        pre,
        sh_feat,
    )
    voxel_total = lax.axis_size("rep") * lax.axis_size("blocks") * BD * 512
    grad_one, grad_two = reduce_all(grads, core, 1.0 / math.sqrt(voxel_total))
    (out,) = call(
        second_kernel,
        [((BD, 512, CH), BF)],
        scratch_own() + scratch_build() + [pltpu.VMEM(SHIFTED, BF)],
        nb,
        dev,
        hid,
        *hid_pieces,
        w_two,
    )
    return out[None], grad_one, grad_two


def solution(mesh):
    in_specs = (
        P("rep", "blocks", None, None),
        P(),
        P(),
        P("rep", "blocks", None, None),
        P("rep", "blocks", None),
    )
    out_specs = (P("rep", "blocks", None, None), P(), P())
    return jax.shard_map(local, mesh=mesh, in_specs=in_specs, out_specs=out_specs, check_vma=False)
```

```python
import math

import jax
import jax.numpy as jnp
from jax import lax
from jax.experimental import pallas as pl
from jax.experimental.pallas import tpu as pltpu
from jax.sharding import PartitionSpec as P


CH = 128
BD = 4
RX, RE, RP = 256, 128, 256
FULL, MID, FAR = RX + RE + 2 * RP, RX + RE, RX
SLOTS = 20

OFFSETS = [
    (dx, dy, dz)
    for dx in (-1, 0, 1)
    for dy in (-1, 0, 1)
    for dz in (-1, 0, 1)
    if (dx, dy, dz) != (0, 0, 0)
]
K_OF = {offset: k for k, offset in enumerate(OFFSETS)}
BF = jnp.bfloat16
F32 = jnp.float32


def pack_field(nb, dev, own, down, up, fields, f):
    ox, oe = f * RX, fields * RX + f * RE
    oj = fields * (RX + RE) + f * RP
    ol = fields * (RX + RE + RP) + f * RP

    def body(b, carry):
        me = dev * BD + b

        def neighbour(offset):
            return nb[b, K_OF[offset]]

        y_hi, y_lo = neighbour((0, 1, 0)), neighbour((0, -1, 0))
        z_hi, z_lo = neighbour((0, 0, 1)), neighbour((0, 0, -1))
        cases = (
            (down, 0, (y_hi >= 0) & (y_hi < me), (z_hi >= 0) & (z_hi < me)),
            (up, 448, jnp.logical_not(y_lo > me), jnp.logical_not(z_lo > me)),
        )
        edges = jnp.concatenate(
            [own[b, pl.ds(js * 8 + ls, 8, stride=64), :] for js in (0, 7) for ls in (0, 7)], axis=0
        ).astype(BF)
        z_low = own[b, pl.ds(0, 64, stride=8), :]
        z_high = own[b, pl.ds(7, 64, stride=8), :]
        y_low = jnp.concatenate([own[b, i * 64 : i * 64 + 8, :] for i in range(8)], axis=0)
        y_high = jnp.concatenate([own[b, i * 64 + 56 : i * 64 + 64, :] for i in range(8)], axis=0)
        for ref, x_row, take_y, take_z in cases:
            ref[pl.ds(pl.multiple_of(ox + b * 64, 64), 64), :] = own[b, x_row : x_row + 64, :].astype(BF)
            ref[pl.ds(pl.multiple_of(oe + b * 32, 32), 32), :] = edges
            ref[pl.ds(pl.multiple_of(oj + b * 64, 64), 64), :] = jnp.where(take_y, y_high, y_low).astype(BF)
            ref[pl.ds(pl.multiple_of(ol + b * 64, 64), 64), :] = jnp.where(take_z, z_high, z_low).astype(BF)
        return carry

    lax.fori_loop(0, BD, body, 0)


def fill_tables(core, pieces, tx, te, tj, tl, fields, f):
    own_down, own_up, d1, u1, d2, u2, d3, u3, v4, near, wide = pieces
    full, mid, far = fields * FULL, fields * MID, fields * FAR
    turn = 2 * core
    plan = [
        (own_down, 0, 10, 4),
        (own_up, 0, 9, 4),
        (d1, 0, 12, 4),
        (u1, 0, 7, 4),
        (d2, 0, 14, 2),
        (u2, 0, 5, 2),
        (d3, 0, 16, 1),
        (u3, 0, 3, 1),
        (v4, 0, 2 + 15 * core, 1),
        (near, 0, 11 - 3 * core, 4),
        (near, full, 13 - turn, 4),
        (near, 2 * full, 8 - turn, 4),
        (wide, 0, 15 - turn, 2),
        (wide, mid, 6 - turn, 2),
        (wide, 2 * mid, 17 - turn, 1),
        (wide, 2 * mid + far, 4 - turn, 1),
    ]
    for ref, base, slot, kind in plan:
        row = base + f * RX
        tx[slot] = ref[row : row + RX, :].astype(F32).reshape(BD, 64, CH)
        if kind >= 2:
            row = base + fields * RX + f * RE
            te[slot] = ref[row : row + RE, :].astype(F32).reshape(BD, 32, CH)
        if kind >= 4:
            row = base + fields * (RX + RE) + f * RP
            tj[slot] = ref[row : row + RP, :].astype(F32).reshape(BD, 64, CH)
            row += fields * RP
            tl[slot] = ref[row : row + RP, :].astype(F32).reshape(BD, 64, CH)


def build_shifted(nb, dev, own, tx, te, tj, tl, cf, lf, rf, sh):
    def block(b, carry):
        me = dev * BD + b

        def source(offset):
            n = nb[b, K_OF[offset]]
            gap = lax.shift_right_logical(jnp.maximum(n, 0), 2) - dev
            slot = jnp.clip(jnp.where(n > me, 10 + gap, 9 + gap), 0, SLOTS - 1)
            return n >= 0, slot, jnp.maximum(n, 0) & 3

        def keep(valid, rows):
            return jnp.where(valid, rows, jnp.zeros_like(rows))

        for i in range(8):
            cf[b, pl.ds((i + 1) * 80 + 8, 64), :] = own[b, pl.ds(i * 64, 64), :]
        for dy, line in ((-1, 0), (1, 9)):
            valid, slot, loc = source((0, dy, 0))
            for i in range(8):
                rows = tj[slot, loc, pl.ds(i * 8, 8), :]
                cf[b, pl.ds((i + 1) * 80 + line * 8, 8), :] = keep(valid, rows)
        for dx, plane in ((-1, 0), (1, 9)):
            valid, slot, loc = source((dx, 0, 0))
            cf[b, pl.ds(plane * 80 + 8, 64), :] = keep(valid, tx[slot, loc])
            for dy, line, j in ((-1, 0, 7), (1, 9, 0)):
                valid, slot, loc = source((dx, dy, 0))
                rows = tx[slot, loc, pl.ds(j * 8, 8), :]
                cf[b, pl.ds(plane * 80 + line * 8, 8), :] = keep(valid, rows)
        for plane in range(10):
            lines = cf[b, pl.ds(plane * 80, 80), :].reshape(10, 8, CH)
            lf[b, pl.ds(plane * 80, 80), :] = pltpu.roll(lines, 1, 1).reshape(80, CH)
            rf[b, pl.ds(plane * 80, 80), :] = pltpu.roll(lines, 7, 1).reshape(80, CH)
        for dz, ref, cell, l in ((-1, lf, 0, 7), (1, rf, 7, 0)):
            valid, slot, loc = source((0, 0, dz))
            for i in range(8):
                rows = tl[slot, loc, pl.ds(i * 8, 8), :]
                ref[b, pl.ds((i + 1) * 80 + 8 + cell, 8, stride=8), :] = keep(valid, rows)
            for dy, line, j in ((-1, 0, 7), (1, 9, 0)):
                valid, slot, loc = source((0, dy, dz))
                edge = (2 * (j // 7) + l // 7) * 8
                rows = te[slot, loc, pl.ds(edge, 8), :]
                ref[b, pl.ds(80 + line * 8 + cell, 8, stride=80), :] = keep(valid, rows)
            for dx, plane in ((-1, 0), (1, 9)):
                valid, slot, loc = source((dx, 0, dz))
                rows = tx[slot, loc, pl.ds(l, 8, stride=8), :]
                ref[b, pl.ds(plane * 80 + 8 + cell, 8, stride=8), :] = keep(valid, rows)
                for dy, line, j in ((-1, 0, 7), (1, 9, 0)):
                    valid, slot, loc = source((dx, dy, dz))
                    rows = tx[slot, loc, pl.ds(j * 8 + l, 1), :]
                    ref[b, pl.ds(plane * 80 + line * 8 + cell, 1), :] = keep(valid, rows)
        return carry

    lax.fori_loop(0, BD, block, 0)

    def join(plane, carry):
        row = pl.multiple_of(plane * 80, 80)
        for pair in range(2):
            for c, ref in ((0, lf), (1, cf), (2, rf)):
                halves = [ref[2 * pair + h, pl.ds(row, 80), :].reshape(10, 8, CH) for h in (0, 1)]
                sh[c, pair, plane] = jnp.concatenate(halves, axis=1).astype(BF)
        return carry

    lax.fori_loop(0, 10, join, 0)


def slabs(sh, pair, first, count, taps):
    return jnp.concatenate(
        [
            sh[c, pair, pl.ds(first + a, count), b : b + 8].reshape(count * 128, CH)
            for a, b, c in taps
        ],
        axis=1,
    )


TAPS = [(a, b, c) for a in range(3) for b in range(3) for c in range(3)]
CHUNK = 4


def conv(sh, weight, emit):
    def body(step, carry):
        pair = step // (8 // CHUNK)
        first = (step % (8 // CHUNK)) * CHUNK
        rows = jnp.dot(slabs(sh, pair, first, CHUNK, TAPS), weight[...], preferred_element_type=F32)
        emit(pair, first, rows)
        return carry

    lax.fori_loop(0, 2 * (8 // CHUNK), body, 0)


def split_blocks(pair, first, rows, store):
    lines = rows.reshape(CHUNK * 8, 16, CH)
    for h in (0, 1):
        part = lines[:, 8 * h : 8 * h + 8].reshape(CHUNK * 64, CH)
        store(2 * pair + h, pl.multiple_of(first * 64, 64), part)


def load_own(ref, own):
    for b in range(BD):
        own[b] = ref[b].astype(F32)


def pack_kernel(nb, dev, feat, cot, down, up, own):
    for f, ref in enumerate((feat, cot)):
        load_own(ref, own)
        pack_field(nb, dev[0], own, down, up, 2, f)


def forward_kernel(nb, dev, feat, *refs):
    pieces, weight = refs[:11], refs[11]
    hid, hid_s, pre, down, up, sh, own, tx, te, tj, tl, cf, lf, rf = refs[12:]
    load_own(feat, own)
    fill_tables(dev[0] & 1, pieces, tx, te, tj, tl, 2, 0)
    build_shifted(nb, dev[0], own, tx, te, tj, tl, cf, lf, rf, sh)

    def emit(pair, first, rows):
        at = pl.ds(pl.multiple_of(pair * 1024 + first * 128, 128), CHUNK * 128)
        pre[at, :] = rows
        act = (rows / (1.0 + jnp.exp(-rows))).astype(BF)
        hid_s[at, :] = act

        def store(b, row, part):
            own[b, pl.ds(row, CHUNK * 64), :] = part
            hid[b, pl.ds(row, CHUNK * 64), :] = part.astype(BF)

        split_blocks(pair, first, act.astype(F32), store)

    conv(sh, weight, emit)
    pack_field(nb, dev[0], own, down, up, 1, 0)


def backward_kernel(nb, dev, cot, *refs):
    pieces, weight, hid_s, pre = refs[:11], refs[11], refs[12], refs[13]
    sh, hid_t, delta_t, own, tx, te, tj, tl, cf, lf, rf, delta = refs[14:]
    load_own(cot, own)
    fill_tables(dev[0] & 1, pieces, tx, te, tj, tl, 2, 1)
    build_shifted(nb, dev[0], own, tx, te, tj, tl, cf, lf, rf, sh)

    def emit(pair, first, rows):
        at = pl.ds(pl.multiple_of(pair * 1024 + first * 128, 128), CHUNK * 128)
        v = pre[at, :]
        sig = 1.0 / (1.0 + jnp.exp(-v))
        delta[at, :] = (rows * (sig * (1.0 + v * (1.0 - sig)))).astype(BF)

    conv(sh, weight, emit)
    for pair in range(2):
        hid_t[pair] = hid_s[pair * 1024 : pair * 1024 + 1024, :].T
        delta_t[pair] = delta[pair * 1024 : pair * 1024 + 1024, :].T


def gradient_kernel(nb, dev, hid_t, delta_t, sh_feat, sh, keep, send):
    def body(step, carry):
        a, b = step // 3, step % 3

        def product(left, ref):
            total = None
            for pair in range(2):
                right = jnp.concatenate(
                    [ref[c, pair, pl.ds(a, 8), pl.ds(b, 8)].reshape(1024, CH) for c in range(3)], axis=1
                )
                term = jnp.dot(left[pair], right, preferred_element_type=F32)
                total = term if total is None else total + term
            return total

        one = product(delta_t, sh_feat)
        two = product(hid_t, sh)

        def write(first, second):
            for c in range(3):
                row = pl.multiple_of((step * 3 + c) * CH, CH)
                first[pl.ds(row, CH), :] = one[:, c * CH : c * CH + CH].T
                row = pl.multiple_of((26 - step * 3 - c) * CH, CH)
                second[pl.ds(row, CH), :] = two[:, c * CH : c * CH + CH]

        @pl.when((dev[0] & 1) == 0)
        def _():
            write(keep, send)

        @pl.when((dev[0] & 1) == 1)
        def _():
            write(send, keep)

        return carry

    lax.fori_loop(0, 9, body, 0)


def second_kernel(nb, dev, hid, *refs):
    pieces, weight, out = refs[:11], refs[11], refs[12]
    own, tx, te, tj, tl, cf, lf, rf, sh = refs[13:]
    load_own(hid, own)
    fill_tables(dev[0] & 1, pieces, tx, te, tj, tl, 1, 0)
    build_shifted(nb, dev[0], own, tx, te, tj, tl, cf, lf, rf, sh)

    def emit(pair, first, rows):
        def store(b, row, part):
            out[b, pl.ds(row, CHUNK * 64), :] = part.astype(BF)

        split_blocks(pair, first, rows, store)

    conv(sh, weight, emit)


def scratch_own():
    return [pltpu.VMEM((BD, 512, CH), F32)]


def scratch_build():
    return [
        pltpu.VMEM((SLOTS, BD, 64, CH), F32),
        pltpu.VMEM((SLOTS, BD, 32, CH), F32),
        pltpu.VMEM((SLOTS, BD, 64, CH), F32),
        pltpu.VMEM((SLOTS, BD, 64, CH), F32),
    ] + [pltpu.VMEM((BD, 800, CH), F32)] * 3


SHIFTED = (3, 2, 10, 10, 16, CH)


def call(kernel, outs, scratch, nb, dev, *arrays):
    smem = pl.BlockSpec(memory_space=pltpu.SMEM)
    vmem = pl.BlockSpec(memory_space=pltpu.VMEM)
    return pl.pallas_call(
        kernel,
        out_shape=[jax.ShapeDtypeStruct(shape, dtype) for shape, dtype in outs],
        in_specs=[smem, smem] + [vmem] * len(arrays),
        out_specs=[vmem] * len(outs),
        scratch_shapes=scratch,
    )(nb, dev, *arrays)


def hop(x, shift):
    size = lax.axis_size("blocks")
    return lax.ppermute(x, "blocks", [(i, (i + shift(i)) % size) for i in range(size)])


def swap(x):
    return hop(x, lambda i: 1 - 2 * (i % 2))


def exchange_near(down, up):
    return hop(down, lambda i: -2), hop(up, lambda i: 2)


def exchange_rest(down, up, d1, u1, fields, core):
    mid, far = fields * MID, fields * FAR
    last = jnp.where(core == 0, d1[:far], u1[:far])
    v4 = hop(last, lambda i: -5 if i % 2 == 0 else 5)
    d3, u3 = hop(d1[:far], lambda i: -4), hop(u1[:far], lambda i: 4)
    d2, u2 = hop(d1[:mid], lambda i: -2), hop(u1[:mid], lambda i: 2)
    mine = jnp.where(core == 0, up, down)
    near = swap(jnp.concatenate([mine, d1, u1], axis=0))
    wide = swap(jnp.concatenate([d2, u2, d3, u3], axis=0))
    return (down, up, d1, u1, d2, u2, d3, u3, v4, near, wide)


def all_to_all(x, axes, groups):
    return lax.all_to_all(x, axes, 0, 0, axis_index_groups=groups, tiled=True)


def reduce_all(keep, send, core, scale, work, given):
    size, reps = lax.axis_size("blocks"), lax.axis_size("rep")
    length = 8
    width = size // (2 * length)
    planes = [
        [(2 * length * x + 2 * z + c) * reps + r for x in range(width) for r in range(reps)]
        for z in range(length)
        for c in range(2)
    ]
    columns = [
        [2 * length * x + 2 * z + c for z in range(length)] for x in range(width) for c in range(2)
    ]
    both = ("blocks", "rep")
    count = width * reps
    rows = keep.shape[0] // count
    mine = keep + swap(send)
    part = all_to_all(mine.astype(BF).reshape(count, rows, CH), both, planes)
    part = jnp.sum(part.astype(F32), axis=0).astype(BF)
    part, given = lax.optimization_barrier((part, given))
    done = work(given)
    part = jnp.broadcast_to(part[None], (length, rows, CH))
    part = all_to_all(part, "blocks", columns)
    part = (jnp.sum(part.astype(F32), axis=0) * scale).astype(BF)
    part, done = lax.optimization_barrier((part, done))
    part = jnp.broadcast_to(part[None], (count, rows, CH))
    mine = all_to_all(part, both, planes).reshape(keep.shape)
    theirs = swap(mine)
    shape = (keep.shape[0] // CH, CH, CH)
    one = jnp.where(core == 0, mine, theirs).astype(F32).reshape(shape)
    two = jnp.where(core == 0, theirs, mine).astype(F32).reshape(shape)
    return one, two, done


def slab_step(features, weight_one, weight_two, cotangent, neighbours):
    feat, cot, nb = features[0], cotangent[0], neighbours[0]
    index = lax.axis_index("blocks")
    core = index % 2
    dev = index.astype(jnp.int32).reshape(1)
    w_one = weight_one.reshape(27 * CH, CH)
    w_two = weight_two.reshape(27 * CH, CH)
    flipped = jnp.transpose(weight_two[::-1], (0, 2, 1)).reshape(27 * CH, CH)
    two_fields = (2 * FULL, CH)
    down, up = call(pack_kernel, [(two_fields, BF)] * 2, scratch_own(), nb, dev, feat, cot)
    d1, u1 = exchange_near(down, up)
    pieces = exchange_rest(down, up, d1, u1, 2, core)
    hid, hid_s, pre, hid_down, hid_up, sh_feat = call(
        forward_kernel,
        [
            ((BD, 512, CH), BF),
            ((BD * 512, CH), BF),
            ((BD * 512, CH), F32),
            ((FULL, CH), BF),
            ((FULL, CH), BF),
            (SHIFTED, BF),
        ],
        scratch_own() + scratch_build(),
        nb,
        dev,
        feat,
        *pieces,
        w_one,
    )
    d1, u1 = exchange_near(hid_down, hid_up)
    sh_cot, hid_t, delta_t = call(
        backward_kernel,
        [(SHIFTED, BF), ((2, CH, 1024), BF), ((2, CH, 1024), BF)],
        scratch_own() + scratch_build() + [pltpu.VMEM((BD * 512, CH), BF)],
        nb,
        dev,
        cot,
        *pieces,
        flipped,
        hid_s,
        pre,
    )
    d1, u1, hid_t, delta_t, sh_cot = lax.optimization_barrier((d1, u1, hid_t, delta_t, sh_cot))
    hid_pieces = exchange_rest(hid_down, hid_up, d1, u1, 1, core)
    keep, send = call(
        gradient_kernel,
        [((27 * CH, CH), F32)] * 2,
        [],
        nb,
        dev,
        hid_t,
        delta_t,
        sh_feat,
        sh_cot,
    )
    (keep, send), hid_pieces = lax.optimization_barrier(((keep, send), hid_pieces))
    voxel_total = lax.axis_size("rep") * lax.axis_size("blocks") * BD * 512
    scale = 1.0 / math.sqrt(voxel_total)

    def second(hid):
        return call(
            second_kernel,
            [((BD, 512, CH), BF)],
            scratch_own() + scratch_build() + [pltpu.VMEM(SHIFTED, BF)],
            nb,
            dev,
            hid,
            *hid_pieces,
            w_two,
        )[0]

    grad_one, grad_two, out = reduce_all(keep, send, core, scale, second, hid)
    return out[None], grad_one, grad_two


def solution(mesh):
    in_specs = (
        P("rep", "blocks", None, None),
        P(),
        P(),
        P("rep", "blocks", None, None),
        P("rep", "blocks", None),
    )
    out_specs = (P("rep", "blocks", None, None), P(), P())
    return jax.shard_map(slab_step, mesh=mesh, in_specs=in_specs, out_specs=out_specs, check_vma=False)
```

```python
import math

import jax
import jax.numpy as jnp
from jax import lax
from jax.experimental import pallas as pl
from jax.experimental.pallas import tpu as pltpu
from jax.sharding import PartitionSpec as P


CH = 128
BD = 4
RX, RE, RP = 256, 128, 256
FULL, MID, FAR = RX + RE + 2 * RP, RX + RE, RX
SLOTS = 20

OFFSETS = [
    (dx, dy, dz)
    for dx in (-1, 0, 1)
    for dy in (-1, 0, 1)
    for dz in (-1, 0, 1)
    if (dx, dy, dz) != (0, 0, 0)
]
K_OF = {offset: k for k, offset in enumerate(OFFSETS)}
BF = jnp.bfloat16
F32 = jnp.float32


def pack_field(nb, dev, own, down, up):
    ox, oe, oj, ol = 0, RX, RX + RE, RX + RE + RP

    def body(b, carry):
        me = dev * BD + b

        def neighbour(offset):
            return nb[b, K_OF[offset]]

        y_hi, y_lo = neighbour((0, 1, 0)), neighbour((0, -1, 0))
        z_hi, z_lo = neighbour((0, 0, 1)), neighbour((0, 0, -1))
        cases = (
            (down, 0, (y_hi >= 0) & (y_hi < me), (z_hi >= 0) & (z_hi < me)),
            (up, 448, jnp.logical_not(y_lo > me), jnp.logical_not(z_lo > me)),
        )
        edges = jnp.concatenate(
            [own[b, pl.ds(js * 8 + ls, 8, stride=64), :] for js in (0, 7) for ls in (0, 7)], axis=0
        ).astype(BF)
        z_low = own[b, pl.ds(0, 64, stride=8), :]
        z_high = own[b, pl.ds(7, 64, stride=8), :]
        y_low = jnp.concatenate([own[b, i * 64 : i * 64 + 8, :] for i in range(8)], axis=0)
        y_high = jnp.concatenate([own[b, i * 64 + 56 : i * 64 + 64, :] for i in range(8)], axis=0)
        for ref, x_row, take_y, take_z in cases:
            ref[pl.ds(pl.multiple_of(ox + b * 64, 64), 64), :] = own[b, x_row : x_row + 64, :].astype(BF)
            ref[pl.ds(pl.multiple_of(oe + b * 32, 32), 32), :] = edges
            ref[pl.ds(pl.multiple_of(oj + b * 64, 64), 64), :] = jnp.where(take_y, y_high, y_low).astype(BF)
            ref[pl.ds(pl.multiple_of(ol + b * 64, 64), 64), :] = jnp.where(take_z, z_high, z_low).astype(BF)
        return carry

    lax.fori_loop(0, BD, body, 0)


def fill_tables(core, pieces, tx, te, tj, tl):
    own_down, own_up, d1, u1, d2, u2, v4, near, wide_d, wide_u = pieces
    turn = 2 * core
    plan = [
        (own_down, 0, 10, 4),
        (own_up, 0, 9, 4),
        (d1, 0, 12, 4),
        (u1, 0, 7, 4),
        (d2, 0, 14, 2),
        (u2, 0, 5, 2),
        (d2, MID, 16, 1),
        (u2, MID, 3, 1),
        (v4, 0, 2 + 15 * core, 1),
        (near, 0, 11 - 3 * core, 4),
        (near, FULL, 13 - turn, 4),
        (near, 2 * FULL, 8 - turn, 4),
        (wide_d, 0, 15 - turn, 2),
        (wide_u, 0, 6 - turn, 2),
        (wide_d, MID, 17 - turn, 1),
        (wide_u, MID, 4 - turn, 1),
    ]
    for ref, row, slot, kind in plan:
        tx[slot] = ref[row : row + RX, :].astype(F32).reshape(BD, 64, CH)
        if kind >= 2:
            row += RX
            te[slot] = ref[row : row + RE, :].astype(F32).reshape(BD, 32, CH)
        if kind >= 4:
            row += RE
            tj[slot] = ref[row : row + RP, :].astype(F32).reshape(BD, 64, CH)
            row += RP
            tl[slot] = ref[row : row + RP, :].astype(F32).reshape(BD, 64, CH)


def build_shifted(nb, dev, own, tx, te, tj, tl, cf, lf, rf, sh):
    def block(b, carry):
        me = dev * BD + b

        def source(offset):
            n = nb[b, K_OF[offset]]
            gap = lax.shift_right_logical(jnp.maximum(n, 0), 2) - dev
            slot = jnp.clip(jnp.where(n > me, 10 + gap, 9 + gap), 0, SLOTS - 1)
            return n >= 0, slot, jnp.maximum(n, 0) & 3

        def keep(valid, rows):
            return jnp.where(valid, rows, jnp.zeros_like(rows))

        for i in range(8):
            cf[b, pl.ds((i + 1) * 80 + 8, 64), :] = own[b, pl.ds(i * 64, 64), :]
        for dy, line in ((-1, 0), (1, 9)):
            valid, slot, loc = source((0, dy, 0))
            for i in range(8):
                rows = tj[slot, loc, pl.ds(i * 8, 8), :]
                cf[b, pl.ds((i + 1) * 80 + line * 8, 8), :] = keep(valid, rows)
        for dx, plane in ((-1, 0), (1, 9)):
            valid, slot, loc = source((dx, 0, 0))
            cf[b, pl.ds(plane * 80 + 8, 64), :] = keep(valid, tx[slot, loc])
            for dy, line, j in ((-1, 0, 7), (1, 9, 0)):
                valid, slot, loc = source((dx, dy, 0))
                rows = tx[slot, loc, pl.ds(j * 8, 8), :]
                cf[b, pl.ds(plane * 80 + line * 8, 8), :] = keep(valid, rows)
        for plane in range(10):
            lines = cf[b, pl.ds(plane * 80, 80), :].reshape(10, 8, CH)
            lf[b, pl.ds(plane * 80, 80), :] = pltpu.roll(lines, 1, 1).reshape(80, CH)
            rf[b, pl.ds(plane * 80, 80), :] = pltpu.roll(lines, 7, 1).reshape(80, CH)
        for dz, ref, cell, l in ((-1, lf, 0, 7), (1, rf, 7, 0)):
            valid, slot, loc = source((0, 0, dz))
            for i in range(8):
                rows = tl[slot, loc, pl.ds(i * 8, 8), :]
                ref[b, pl.ds((i + 1) * 80 + 8 + cell, 8, stride=8), :] = keep(valid, rows)
            for dy, line, j in ((-1, 0, 7), (1, 9, 0)):
                valid, slot, loc = source((0, dy, dz))
                edge = (2 * (j // 7) + l // 7) * 8
                rows = te[slot, loc, pl.ds(edge, 8), :]
                ref[b, pl.ds(80 + line * 8 + cell, 8, stride=80), :] = keep(valid, rows)
            for dx, plane in ((-1, 0), (1, 9)):
                valid, slot, loc = source((dx, 0, dz))
                rows = tx[slot, loc, pl.ds(l, 8, stride=8), :]
                ref[b, pl.ds(plane * 80 + 8 + cell, 8, stride=8), :] = keep(valid, rows)
                for dy, line, j in ((-1, 0, 7), (1, 9, 0)):
                    valid, slot, loc = source((dx, dy, dz))
                    rows = tx[slot, loc, pl.ds(j * 8 + l, 1), :]
                    ref[b, pl.ds(plane * 80 + line * 8 + cell, 1), :] = keep(valid, rows)
        return carry

    lax.fori_loop(0, BD, block, 0)

    def join(plane, carry):
        row = pl.multiple_of(plane * 80, 80)
        for pair in range(2):
            for c, ref in ((0, lf), (1, cf), (2, rf)):
                halves = [ref[2 * pair + h, pl.ds(row, 80), :].reshape(10, 8, CH) for h in (0, 1)]
                sh[c, pair, plane] = jnp.concatenate(halves, axis=1).astype(BF)
        return carry

    lax.fori_loop(0, 10, join, 0)


def slabs(sh, pair, first, count, taps):
    return jnp.concatenate(
        [
            sh[c, pair, pl.ds(first + a, count), b : b + 8].reshape(count * 128, CH)
            for a, b, c in taps
        ],
        axis=1,
    )


TAPS = [(a, b, c) for a in range(3) for b in range(3) for c in range(3)]
CHUNK = 4


def conv(sh, weight, emit):
    def body(step, carry):
        pair = step // (8 // CHUNK)
        first = (step % (8 // CHUNK)) * CHUNK
        rows = jnp.dot(slabs(sh, pair, first, CHUNK, TAPS), weight[...], preferred_element_type=F32)
        emit(pair, first, rows)
        return carry

    lax.fori_loop(0, 2 * (8 // CHUNK), body, 0)


def split_blocks(pair, first, rows, store):
    lines = rows.reshape(CHUNK * 8, 16, CH)
    for h in (0, 1):
        part = lines[:, 8 * h : 8 * h + 8].reshape(CHUNK * 64, CH)
        store(2 * pair + h, pl.multiple_of(first * 64, 64), part)


def load_own(ref, own):
    for b in range(BD):
        own[b] = ref[b].astype(F32)


def pack_kernel(nb, dev, field, down, up, own):
    load_own(field, own)
    pack_field(nb, dev[0], own, down, up)


def forward_kernel(nb, dev, feat, *refs):
    pieces, weight = refs[:10], refs[10]
    hid, hid_s, pre, down, up, sh, own, tx, te, tj, tl, cf, lf, rf = refs[11:]
    load_own(feat, own)
    fill_tables(dev[0] & 1, pieces, tx, te, tj, tl)
    build_shifted(nb, dev[0], own, tx, te, tj, tl, cf, lf, rf, sh)

    def emit(pair, first, rows):
        at = pl.ds(pl.multiple_of(pair * 1024 + first * 128, 128), CHUNK * 128)
        pre[at, :] = rows
        act = (rows / (1.0 + jnp.exp(-rows))).astype(BF)
        hid_s[at, :] = act

        def store(b, row, part):
            own[b, pl.ds(row, CHUNK * 64), :] = part
            hid[b, pl.ds(row, CHUNK * 64), :] = part.astype(BF)

        split_blocks(pair, first, act.astype(F32), store)

    conv(sh, weight, emit)
    pack_field(nb, dev[0], own, down, up)


def backward_kernel(nb, dev, cot, *refs):
    pieces, weight, hid_s, pre = refs[:10], refs[10], refs[11], refs[12]
    sh, hid_t, delta_t, own, tx, te, tj, tl, cf, lf, rf, delta = refs[13:]
    load_own(cot, own)
    fill_tables(dev[0] & 1, pieces, tx, te, tj, tl)
    build_shifted(nb, dev[0], own, tx, te, tj, tl, cf, lf, rf, sh)

    def emit(pair, first, rows):
        at = pl.ds(pl.multiple_of(pair * 1024 + first * 128, 128), CHUNK * 128)
        v = pre[at, :]
        sig = 1.0 / (1.0 + jnp.exp(-v))
        delta[at, :] = (rows * (sig * (1.0 + v * (1.0 - sig)))).astype(BF)

    conv(sh, weight, emit)
    for pair in range(2):
        at = slice(pair * 1024, pair * 1024 + 1024)
        hid_t[:, at] = hid_s[at, :].T
        delta_t[:, at] = delta[at, :].T


def gradient_kernel(nb, dev, hid_t, delta_t, sh_feat, sh, keep, send):
    def body(a, carry):
        def product(left, ref):
            right = jnp.concatenate(
                [
                    jnp.concatenate(
                        [ref[c, pair, pl.ds(a, 8), b : b + 8].reshape(1024, CH) for b in range(3) for c in range(3)],
                        axis=1,
                    )
                    for pair in range(2)
                ],
                axis=0,
            )
            return jnp.dot(left[...], right, preferred_element_type=F32)

        def write(first, second):
            one = product(delta_t, sh_feat)
            for t in range(9):
                row = pl.multiple_of((a * 9 + t) * CH, CH)
                first[pl.ds(row, CH), :] = one[:, t * CH : t * CH + CH].T
            two = product(hid_t, sh)
            for t in range(9):
                row = pl.multiple_of((26 - a * 9 - t) * CH, CH)
                second[pl.ds(row, CH), :] = two[:, t * CH : t * CH + CH]

        @pl.when((dev[0] & 1) == 0)
        def _():
            write(keep, send)

        @pl.when((dev[0] & 1) == 1)
        def _():
            write(send, keep)

        return carry

    lax.fori_loop(0, 3, body, 0)


def second_kernel(nb, dev, hid, *refs):
    pieces, weight, out = refs[:10], refs[10], refs[11]
    own, tx, te, tj, tl, cf, lf, rf, sh = refs[12:]
    load_own(hid, own)
    fill_tables(dev[0] & 1, pieces, tx, te, tj, tl)
    build_shifted(nb, dev[0], own, tx, te, tj, tl, cf, lf, rf, sh)

    def emit(pair, first, rows):
        def store(b, row, part):
            out[b, pl.ds(row, CHUNK * 64), :] = part.astype(BF)

        split_blocks(pair, first, rows, store)

    conv(sh, weight, emit)


def scratch_own():
    return [pltpu.VMEM((BD, 512, CH), F32)]


def scratch_build():
    return [
        pltpu.VMEM((SLOTS, BD, 64, CH), F32),
        pltpu.VMEM((SLOTS, BD, 32, CH), F32),
        pltpu.VMEM((SLOTS, BD, 64, CH), F32),
        pltpu.VMEM((SLOTS, BD, 64, CH), F32),
    ] + [pltpu.VMEM((BD, 800, CH), F32)] * 3


SHIFTED = (3, 2, 10, 10, 16, CH)
LIMIT = 36


def call(kernel, outs, scratch, nb, dev, *arrays, limit=LIMIT):
    smem = pl.BlockSpec(memory_space=pltpu.SMEM)
    vmem = pl.BlockSpec(memory_space=pltpu.VMEM)
    return pl.pallas_call(
        kernel,
        out_shape=[jax.ShapeDtypeStruct(shape, dtype) for shape, dtype in outs],
        in_specs=[smem, smem] + [vmem] * len(arrays),
        out_specs=[vmem] * len(outs),
        scratch_shapes=scratch,
        compiler_params=pltpu.CompilerParams(vmem_limit_bytes=limit << 20),
    )(nb, dev, *arrays)


def hop(x, shift):
    size = lax.axis_size("blocks")
    return lax.ppermute(x, "blocks", [(i, (i + shift(i)) % size) for i in range(size)])


def swap(x):
    return hop(x, lambda i: 1 - 2 * (i % 2))


def exchange_near(down, up):
    return hop(down, lambda i: -2), hop(up, lambda i: 2)


def forward_planes(nb, dev, down, up, d1, u1, far_down, far_up, last, near):
    for own, got, out in ((down, d1, far_down), (up, u1, far_up)):
        out[0:MID, :] = own[0:MID, :]
        out[MID : MID + FAR, :] = got[0:FAR, :]
    near[FULL : 2 * FULL, :] = d1[...]
    near[2 * FULL : 3 * FULL, :] = u1[...]
    first = (dev[0] & 1) == 0

    @pl.when(first)
    def _():
        last[...] = d1[0:FAR, :]
        near[0:FULL, :] = up[...]

    @pl.when(jnp.logical_not(first))
    def _():
        last[...] = u1[0:FAR, :]
        near[0:FULL, :] = down[...]


def exchange_far(nb, dev, down, up, d1, u1):
    outs = [((MID + FAR, CH), BF)] * 2 + [((FAR, CH), BF), ((3 * FULL, CH), BF)]
    far_down, far_up, last, near = call(forward_planes, outs, [], nb, dev, down, up, d1, u1, limit=8)
    v4 = hop(last, lambda i: -5 if i % 2 == 0 else 5)
    d2 = hop(far_down, lambda i: -4)
    u2 = hop(far_up, lambda i: 4)
    return d2, u2, v4, swap(near)


def exchange_wide(d2, u2):
    return swap(d2), swap(u2)


def all_to_all(x, axes, groups):
    return lax.all_to_all(x, axes, 0, 0, axis_index_groups=groups, tiled=True)


def reduce_all(keep, send, core, scale, work, given):
    size, reps = lax.axis_size("blocks"), lax.axis_size("rep")
    length = 8
    width = size // (2 * length)
    planes = [
        [(2 * length * x + 2 * z + c) * reps + r for x in range(width) for r in range(reps)]
        for z in range(length)
        for c in range(2)
    ]
    columns = [
        [2 * length * x + 2 * z + c for z in range(length)] for x in range(width) for c in range(2)
    ]
    both = ("blocks", "rep")
    count = width * reps
    rows = keep.shape[0] // count
    mine = keep + swap(send)
    part = all_to_all(mine.astype(BF).reshape(count, rows, CH), both, planes)
    part = jnp.sum(part.astype(F32), axis=0).astype(BF)
    part, given = lax.optimization_barrier((part, given))
    done = work(given)
    part = jnp.broadcast_to(part[None], (length, rows, CH))
    part = all_to_all(part, "blocks", columns)
    part = (jnp.sum(part.astype(F32), axis=0) * scale).astype(BF)
    part, done = lax.optimization_barrier((part, done))
    part = jnp.broadcast_to(part[None], (count, rows, CH))
    mine = all_to_all(part, both, planes).reshape(keep.shape)
    theirs = swap(mine)
    shape = (keep.shape[0] // CH, CH, CH)
    one = jnp.where(core == 0, mine, theirs).astype(F32).reshape(shape)
    two = jnp.where(core == 0, theirs, mine).astype(F32).reshape(shape)
    return one, two, done


def slab_step(features, weight_one, weight_two, cotangent, neighbours):
    feat, cot, nb = features[0], cotangent[0], neighbours[0]
    index = lax.axis_index("blocks")
    core = index % 2
    dev = index.astype(jnp.int32).reshape(1)
    w_one = weight_one.reshape(27 * CH, CH)
    w_two = weight_two.reshape(27 * CH, CH)
    flipped = jnp.transpose(weight_two[::-1], (0, 2, 1)).reshape(27 * CH, CH)
    halo = [((FULL, CH), BF)] * 2
    f_down, f_up = call(pack_kernel, halo, scratch_own(), nb, dev, feat)
    f_d1, f_u1 = exchange_near(f_down, f_up)
    c_down, c_up = call(pack_kernel, halo, scratch_own(), nb, dev, cot)
    c_d1, c_u1 = exchange_near(c_down, c_up)
    f_d1, f_u1, flipped = lax.optimization_barrier((f_d1, f_u1, flipped))
    f_far = exchange_far(nb, dev, f_down, f_up, f_d1, f_u1)
    c_far = exchange_far(nb, dev, c_down, c_up, c_d1, c_u1)
    pieces = (f_down, f_up, f_d1, f_u1, *f_far, *exchange_wide(f_far[0], f_far[1]))
    hid, hid_s, pre, hid_down, hid_up, sh_feat = call(
        forward_kernel,
        [
            ((BD, 512, CH), BF),
            ((BD * 512, CH), BF),
            ((BD * 512, CH), F32),
            ((FULL, CH), BF),
            ((FULL, CH), BF),
            (SHIFTED, BF),
        ],
        scratch_own() + scratch_build(),
        nb,
        dev,
        feat,
        *pieces,
        w_one,
    )
    c_far, hid_down, hid_up = lax.optimization_barrier((c_far, hid_down, hid_up))
    d1, u1 = exchange_near(hid_down, hid_up)
    pieces = (c_down, c_up, c_d1, c_u1, *c_far, *exchange_wide(c_far[0], c_far[1]))
    sh_cot, hid_t, delta_t = call(
        backward_kernel,
        [(SHIFTED, BF), ((CH, BD * 512), BF), ((CH, BD * 512), BF)],
        scratch_own() + scratch_build() + [pltpu.VMEM((BD * 512, CH), BF)],
        nb,
        dev,
        cot,
        *pieces,
        flipped,
        hid_s,
        pre,
    )
    d1, u1, hid_t, delta_t, sh_cot = lax.optimization_barrier((d1, u1, hid_t, delta_t, sh_cot))
    h_far = exchange_far(nb, dev, hid_down, hid_up, d1, u1)
    keep, send = call(
        gradient_kernel,
        [((27 * CH, CH), F32)] * 2,
        [],
        nb,
        dev,
        hid_t,
        delta_t,
        sh_feat,
        sh_cot,
    )
    (keep, send), h_far = lax.optimization_barrier(((keep, send), h_far))
    hid_pieces = (hid_down, hid_up, d1, u1, *h_far, *exchange_wide(h_far[0], h_far[1]))
    voxel_total = lax.axis_size("rep") * lax.axis_size("blocks") * BD * 512
    scale = 1.0 / math.sqrt(voxel_total)

    def second(hid):
        return call(
            second_kernel,
            [((BD, 512, CH), BF)],
            scratch_own() + scratch_build() + [pltpu.VMEM(SHIFTED, BF)],
            nb,
            dev,
            hid,
            *hid_pieces,
            w_two,
        )[0]

    grad_one, grad_two, out = reduce_all(keep, send, core, scale, second, hid)
    return out[None], grad_one, grad_two


def solution(mesh):
    in_specs = (
        P("rep", "blocks", None, None),
        P(),
        P(),
        P("rep", "blocks", None, None),
        P("rep", "blocks", None),
    )
    out_specs = (P("rep", "blocks", None, None), P(), P())
    return jax.shard_map(slab_step, mesh=mesh, in_specs=in_specs, out_specs=out_specs, check_vma=False)
```

```python
import functools
import math

import jax
import jax.numpy as jnp
from jax import lax
from jax.experimental import pallas as pl
from jax.experimental.pallas import tpu as pltpu
from jax.sharding import PartitionSpec as P


CH = 128
BD = 4
RX, RE, RP = 256, 128, 256
FULL, MID, FAR = RX + RE + 2 * RP, RX + RE, RX
SLOTS = 20

OFFSETS = [
    (dx, dy, dz)
    for dx in (-1, 0, 1)
    for dy in (-1, 0, 1)
    for dz in (-1, 0, 1)
    if (dx, dy, dz) != (0, 0, 0)
]
K_OF = {offset: k for k, offset in enumerate(OFFSETS)}
BF = jnp.bfloat16
F32 = jnp.float32


def pack_field(nb, dev, own, down, up, last, f):
    ox = f * FULL
    oe, oj, ol = ox + RX, ox + RX + RE, ox + RX + RE + RP

    def body(b, carry):
        me = dev * BD + b

        def neighbour(offset):
            return nb[b, K_OF[offset]]

        y_hi, y_lo = neighbour((0, 1, 0)), neighbour((0, -1, 0))
        z_hi, z_lo = neighbour((0, 0, 1)), neighbour((0, 0, -1))
        cases = (
            (down, 0, (y_hi >= 0) & (y_hi < me), (z_hi >= 0) & (z_hi < me)),
            (up, 448, jnp.logical_not(y_lo > me), jnp.logical_not(z_lo > me)),
        )
        edges = jnp.concatenate(
            [own[b, pl.ds(js * 8 + ls, 8, stride=64), :] for js in (0, 7) for ls in (0, 7)], axis=0
        ).astype(BF)
        z_low = own[b, pl.ds(0, 64, stride=8), :]
        z_high = own[b, pl.ds(7, 64, stride=8), :]
        y_low = jnp.concatenate([own[b, i * 64 : i * 64 + 8, :] for i in range(8)], axis=0)
        y_high = jnp.concatenate([own[b, i * 64 + 56 : i * 64 + 64, :] for i in range(8)], axis=0)
        for ref, x_row, take_y, take_z in cases:
            ref[pl.ds(pl.multiple_of(ox + b * 64, 64), 64), :] = own[b, x_row : x_row + 64, :].astype(BF)
            ref[pl.ds(pl.multiple_of(oe + b * 32, 32), 32), :] = edges
            ref[pl.ds(pl.multiple_of(oj + b * 64, 64), 64), :] = jnp.where(take_y, y_high, y_low).astype(BF)
            ref[pl.ds(pl.multiple_of(ol + b * 64, 64), 64), :] = jnp.where(take_z, z_high, z_low).astype(BF)
        return carry

    lax.fori_loop(0, BD, body, 0)
    first = (dev & 1) == 0

    @pl.when(first)
    def _():
        last[f * FAR : f * FAR + FAR, :] = down[ox : ox + FAR, :]

    @pl.when(jnp.logical_not(first))
    def _():
        last[f * FAR : f * FAR + FAR, :] = up[ox : ox + FAR, :]


def fill_tables(core, pieces, tx, te, tj, tl, fields=1, f=0):
    own_down, own_up, d1, u1, v4, d2, u2, near, wide_d, wide_u = pieces
    turn = 2 * core
    full, two = f * FULL, f * (MID + FAR)
    plan = [
        (own_down, full, 10, 4),
        (own_up, full, 9, 4),
        (d1, full, 12, 4),
        (u1, full, 7, 4),
        (d2, two, 14, 2),
        (u2, two, 5, 2),
        (d2, two + MID, 16, 1),
        (u2, two + MID, 3, 1),
        (v4, f * FAR, 2 + 15 * core, 1),
        (near, full, 11 - 3 * core, 4),
        (near, full + fields * FULL, 13 - turn, 4),
        (near, full + 2 * fields * FULL, 8 - turn, 4),
        (wide_d, two, 15 - turn, 2),
        (wide_u, two, 6 - turn, 2),
        (wide_d, two + MID, 17 - turn, 1),
        (wide_u, two + MID, 4 - turn, 1),
    ]
    for ref, row, slot, kind in plan:
        tx[slot] = ref[row : row + RX, :].astype(F32).reshape(BD, 64, CH)
        if kind >= 2:
            row += RX
            te[slot] = ref[row : row + RE, :].astype(F32).reshape(BD, 32, CH)
        if kind >= 4:
            row += RE
            tj[slot] = ref[row : row + RP, :].astype(F32).reshape(BD, 64, CH)
            row += RP
            tl[slot] = ref[row : row + RP, :].astype(F32).reshape(BD, 64, CH)


def build_shifted(nb, dev, own, tx, te, tj, tl, cf, lf, rf, sh):
    def block(b, carry):
        me = dev * BD + b

        def source(offset):
            n = nb[b, K_OF[offset]]
            gap = lax.shift_right_logical(jnp.maximum(n, 0), 2) - dev
            slot = jnp.clip(jnp.where(n > me, 10 + gap, 9 + gap), 0, SLOTS - 1)
            return n >= 0, slot, jnp.maximum(n, 0) & 3

        def keep(valid, rows):
            return jnp.where(valid, rows, jnp.zeros_like(rows))

        for i in range(8):
            cf[b, pl.ds((i + 1) * 80 + 8, 64), :] = own[b, pl.ds(i * 64, 64), :]
        for dy, line in ((-1, 0), (1, 9)):
            valid, slot, loc = source((0, dy, 0))
            for i in range(8):
                rows = tj[slot, loc, pl.ds(i * 8, 8), :]
                cf[b, pl.ds((i + 1) * 80 + line * 8, 8), :] = keep(valid, rows)
        for dx, plane in ((-1, 0), (1, 9)):
            valid, slot, loc = source((dx, 0, 0))
            cf[b, pl.ds(plane * 80 + 8, 64), :] = keep(valid, tx[slot, loc])
            for dy, line, j in ((-1, 0, 7), (1, 9, 0)):
                valid, slot, loc = source((dx, dy, 0))
                rows = tx[slot, loc, pl.ds(j * 8, 8), :]
                cf[b, pl.ds(plane * 80 + line * 8, 8), :] = keep(valid, rows)
        for plane in range(10):
            lines = cf[b, pl.ds(plane * 80, 80), :].reshape(10, 8, CH)
            lf[b, pl.ds(plane * 80, 80), :] = pltpu.roll(lines, 1, 1).reshape(80, CH)
            rf[b, pl.ds(plane * 80, 80), :] = pltpu.roll(lines, 7, 1).reshape(80, CH)
        for dz, ref, cell, l in ((-1, lf, 0, 7), (1, rf, 7, 0)):
            valid, slot, loc = source((0, 0, dz))
            for i in range(8):
                rows = tl[slot, loc, pl.ds(i * 8, 8), :]
                ref[b, pl.ds((i + 1) * 80 + 8 + cell, 8, stride=8), :] = keep(valid, rows)
            for dy, line, j in ((-1, 0, 7), (1, 9, 0)):
                valid, slot, loc = source((0, dy, dz))
                edge = (2 * (j // 7) + l // 7) * 8
                rows = te[slot, loc, pl.ds(edge, 8), :]
                ref[b, pl.ds(80 + line * 8 + cell, 8, stride=80), :] = keep(valid, rows)
            for dx, plane in ((-1, 0), (1, 9)):
                valid, slot, loc = source((dx, 0, dz))
                rows = tx[slot, loc, pl.ds(l, 8, stride=8), :]
                ref[b, pl.ds(plane * 80 + 8 + cell, 8, stride=8), :] = keep(valid, rows)
                for dy, line, j in ((-1, 0, 7), (1, 9, 0)):
                    valid, slot, loc = source((dx, dy, dz))
                    rows = tx[slot, loc, pl.ds(j * 8 + l, 1), :]
                    ref[b, pl.ds(plane * 80 + line * 8 + cell, 1), :] = keep(valid, rows)
        return carry

    lax.fori_loop(0, BD, block, 0)

    def join(plane, carry):
        row = pl.multiple_of(plane * 80, 80)
        for pair in range(2):
            for c, ref in ((0, lf), (1, cf), (2, rf)):
                halves = [ref[2 * pair + h, pl.ds(row, 80), :].reshape(10, 8, CH) for h in (0, 1)]
                sh[c, pair, plane] = jnp.concatenate(halves, axis=1).astype(BF)
        return carry

    lax.fori_loop(0, 10, join, 0)


def slabs(sh, pair, first, count, taps):
    return jnp.concatenate(
        [
            sh[c, pair, pl.ds(first + a, count), b : b + 8].reshape(count * 128, CH)
            for a, b, c in taps
        ],
        axis=1,
    )


TAPS = [(a, b, c) for a in range(3) for b in range(3) for c in range(3)]
CHUNK = 4


def conv(sh, weight, emit):
    def body(step, carry):
        pair = step // (8 // CHUNK)
        first = (step % (8 // CHUNK)) * CHUNK
        rows = jnp.dot(slabs(sh, pair, first, CHUNK, TAPS), weight[...], preferred_element_type=F32)
        emit(pair, first, rows)
        return carry

    lax.fori_loop(0, 2 * (8 // CHUNK), body, 0)


def split_blocks(pair, first, rows, store):
    lines = rows.reshape(CHUNK * 8, 16, CH)
    for h in (0, 1):
        part = lines[:, 8 * h : 8 * h + 8].reshape(CHUNK * 64, CH)
        store(2 * pair + h, pl.multiple_of(first * 64, 64), part)


def load_own(ref, own):
    for b in range(BD):
        own[b] = ref[b].astype(F32)


def pack_kernel(nb, dev, field, down, up, last, own):
    load_own(field, own)
    pack_field(nb, dev[0], own, down, up, last, 0)


def flip_kernel(nb, dev, weight, out):
    for t in range(27):
        out[t * CH : t * CH + CH, :] = weight[(26 - t) * CH : (27 - t) * CH, :].T


def forward_kernel(nb, dev, feat, *refs):
    pieces, weight = refs[:10], refs[10]
    hid, hid_s, pre, down, up, last, sh, own, tx, te, tj, tl, cf, lf, rf = refs[11:]
    load_own(feat, own)
    fill_tables(dev[0] & 1, pieces, tx, te, tj, tl)
    build_shifted(nb, dev[0], own, tx, te, tj, tl, cf, lf, rf, sh)

    def emit(pair, first, rows):
        at = pl.ds(pl.multiple_of(pair * 1024 + first * 128, 128), CHUNK * 128)
        pre[at, :] = rows
        act = (rows / (1.0 + jnp.exp(-rows))).astype(BF)
        hid_s[at, :] = act

        def store(b, row, part):
            own[b, pl.ds(row, CHUNK * 64), :] = part
            hid[b, pl.ds(row, CHUNK * 64), :] = part.astype(BF)

        split_blocks(pair, first, act.astype(F32), store)

    conv(sh, weight, emit)
    pack_field(nb, dev[0], own, down, up, last, 0)


def backward_kernel(nb, dev, cot, *refs):
    pieces, weight, hid_s, pre = refs[:10], refs[10], refs[11], refs[12]
    sh, hid_t, delta_t, own, tx, te, tj, tl, cf, lf, rf, delta = refs[13:]
    load_own(cot, own)
    fill_tables(dev[0] & 1, pieces, tx, te, tj, tl)
    build_shifted(nb, dev[0], own, tx, te, tj, tl, cf, lf, rf, sh)

    def emit(pair, first, rows):
        at = pl.ds(pl.multiple_of(pair * 1024 + first * 128, 128), CHUNK * 128)
        v = pre[at, :]
        sig = 1.0 / (1.0 + jnp.exp(-v))
        delta[at, :] = (rows * (sig * (1.0 + v * (1.0 - sig)))).astype(BF)

    conv(sh, weight, emit)
    for pair in range(2):
        at = slice(pair * 1024, pair * 1024 + 1024)
        hid_t[:, at] = hid_s[at, :].T
        delta_t[:, at] = delta[at, :].T


def gradient_kernel(nb, dev, hid_t, delta_t, sh_feat, sh, keep, send):
    def body(a, carry):
        def product(left, ref):
            right = jnp.concatenate(
                [
                    jnp.concatenate(
                        [ref[c, pair, pl.ds(a, 8), b : b + 8].reshape(1024, CH) for b in range(3) for c in range(3)],
                        axis=1,
                    )
                    for pair in range(2)
                ],
                axis=0,
            )
            return jnp.dot(left[...], right, preferred_element_type=F32)

        def write(first, second):
            one = product(delta_t, sh_feat)
            for t in range(9):
                row = pl.multiple_of((a * 9 + t) * CH, CH)
                first[pl.ds(row, CH), :] = one[:, t * CH : t * CH + CH].T
            two = product(hid_t, sh)
            for t in range(9):
                row = pl.multiple_of((26 - a * 9 - t) * CH, CH)
                second[pl.ds(row, CH), :] = two[:, t * CH : t * CH + CH]

        @pl.when((dev[0] & 1) == 0)
        def _():
            write(keep, send)

        @pl.when((dev[0] & 1) == 1)
        def _():
            write(send, keep)

        return carry

    lax.fori_loop(0, 3, body, 0)


def second_kernel(nb, dev, hid, *refs):
    pieces, weight, out = refs[:10], refs[10], refs[11]
    own, tx, te, tj, tl, cf, lf, rf, sh = refs[12:]
    load_own(hid, own)
    fill_tables(dev[0] & 1, pieces, tx, te, tj, tl)
    build_shifted(nb, dev[0], own, tx, te, tj, tl, cf, lf, rf, sh)

    def emit(pair, first, rows):
        def store(b, row, part):
            out[b, pl.ds(row, CHUNK * 64), :] = part.astype(BF)

        split_blocks(pair, first, rows, store)

    conv(sh, weight, emit)


def scratch_own():
    return [pltpu.VMEM((BD, 512, CH), F32)]


def scratch_build():
    return [
        pltpu.VMEM((SLOTS, BD, 64, CH), F32),
        pltpu.VMEM((SLOTS, BD, 32, CH), F32),
        pltpu.VMEM((SLOTS, BD, 64, CH), F32),
        pltpu.VMEM((SLOTS, BD, 64, CH), F32),
    ] + [pltpu.VMEM((BD, 800, CH), F32)] * 3


SHIFTED = (3, 2, 10, 10, 16, CH)
LIMIT = 26


def call(kernel, outs, scratch, nb, dev, *arrays, limit=LIMIT):
    smem = pl.BlockSpec(memory_space=pltpu.SMEM)
    vmem = pl.BlockSpec(memory_space=pltpu.VMEM)
    return pl.pallas_call(
        kernel,
        out_shape=[jax.ShapeDtypeStruct(shape, dtype) for shape, dtype in outs],
        in_specs=[smem, smem] + [vmem] * len(arrays),
        out_specs=[vmem] * len(outs),
        scratch_shapes=scratch,
        compiler_params=pltpu.CompilerParams(vmem_limit_bytes=limit << 20),
    )(nb, dev, *arrays)


def hop(x, shift):
    size = lax.axis_size("blocks")
    return lax.ppermute(x, "blocks", [(i, (i + shift(i)) % size) for i in range(size)])


def swap(x):
    return hop(x, lambda i: 1 - 2 * (i % 2))


def exchange_near(down, up, last):
    d1, u1 = hop(down, lambda i: -2), hop(up, lambda i: 2)
    if last is None:
        return d1, u1, None
    return d1, u1, hop(last, lambda i: -7 if i % 2 == 0 else 7)


def forward_planes(fields, nb, dev, down, up, d1, u1, far_down, far_up, near, last):
    full = fields * FULL
    for own, got, out in ((down, d1, far_down), (up, u1, far_up)):
        for f in range(fields):
            at, row = f * (MID + FAR), f * FULL
            out[at : at + MID, :] = own[row : row + MID, :]
            out[at + MID : at + MID + FAR, :] = got[row : row + FAR, :]
    near[full : 2 * full, :] = d1[...]
    near[2 * full : 3 * full, :] = u1[...]
    first = (dev[0] & 1) == 0

    @pl.when(first)
    def _():
        near[0:full, :] = up[...]
        last[...] = d1[0:FAR, :]

    @pl.when(jnp.logical_not(first))
    def _():
        near[0:full, :] = down[...]
        last[...] = u1[0:FAR, :]


def exchange_far(nb, dev, down, up, d1, u1, fields, diagonal=False):
    outs = [((fields * (MID + FAR), CH), BF)] * 2 + [((3 * fields * FULL, CH), BF), ((FAR, CH), BF)]
    kernel = functools.partial(forward_planes, fields)
    far_down, far_up, near, last = call(kernel, outs, [], nb, dev, down, up, d1, u1, limit=8)
    v4 = hop(last, lambda i: -5 if i % 2 == 0 else 5) if diagonal else None
    d2 = hop(far_down, lambda i: -4)
    u2 = hop(far_up, lambda i: 4)
    return d2, u2, swap(near), v4


def exchange_wide(d2, u2):
    return swap(d2), swap(u2)


def sum_kernel(scale, nb, dev, parts, out):
    total = parts[0].astype(F32)
    for k in range(1, parts.shape[0]):
        total = total + parts[k].astype(F32)
    if scale is not None:
        total = total * scale
    total = total.astype(BF)
    for k in range(out.shape[0]):
        out[k] = total


def sum_and_spread(parts, copies, scale, nb, dev):
    kernel = functools.partial(sum_kernel, scale)
    return call(kernel, [((copies, *parts.shape[1:]), BF)], [], nb, dev, parts, limit=8)[0]


def all_to_all(x, axes, groups):
    return lax.all_to_all(x, axes, 0, 0, axis_index_groups=groups, tiled=True)


def reduce_all(keep, send, core, scale, work, given, nb, dev):
    size, reps = lax.axis_size("blocks"), lax.axis_size("rep")
    length = 8
    width = size // (2 * length)
    planes = [
        [(2 * length * x + 2 * z + c) * reps + r for x in range(width) for r in range(reps)]
        for z in range(length)
        for c in range(2)
    ]
    columns = [
        [2 * length * x + 2 * z + c for z in range(length)] for x in range(width) for c in range(2)
    ]
    both = ("blocks", "rep")
    count = width * reps
    rows = keep.shape[0] // count
    mine = keep + swap(send)
    part = all_to_all(mine.astype(BF).reshape(count, rows, CH), both, planes)
    part = sum_and_spread(part, length, None, nb, dev)
    part, given = lax.optimization_barrier((part, given))
    done = work(given)
    part = sum_and_spread(all_to_all(part, "blocks", columns), count, scale, nb, dev)
    part, done = lax.optimization_barrier((part, done))
    mine = all_to_all(part, both, planes).reshape(keep.shape)
    theirs = swap(mine)
    shape = (keep.shape[0] // CH, CH, CH)
    one = jnp.where(core == 0, mine, theirs).astype(F32).reshape(shape)
    two = jnp.where(core == 0, theirs, mine).astype(F32).reshape(shape)
    return one, two, done


def slab_step(features, weight_one, weight_two, cotangent, neighbours):
    feat, cot, nb = features[0], cotangent[0], neighbours[0]
    index = lax.axis_index("blocks")
    core = index % 2
    dev = index.astype(jnp.int32).reshape(1)
    w_one = weight_one.reshape(27 * CH, CH)
    w_two = weight_two.reshape(27 * CH, CH)

    def halo(fields):
        return [((fields * FULL, CH), BF)] * 2 + [((fields * FAR, CH), BF)]

    down, up, _ = call(pack_kernel, halo(1), scratch_own(), nb, dev, feat)
    d1, u1, _ = exchange_near(down, up, None)
    c_down, c_up, _ = call(pack_kernel, halo(1), scratch_own(), nb, dev, cot)
    c_d1, c_u1, _ = exchange_near(c_down, c_up, None)
    (flipped,) = call(flip_kernel, [((27 * CH, CH), BF)], [], nb, dev, w_two, limit=8)
    d1, u1, flipped = lax.optimization_barrier((d1, u1, flipped))
    d2, u2, near, v4 = exchange_far(nb, dev, down, up, d1, u1, 1, True)
    c_d2, c_u2, c_near, c_v4 = exchange_far(nb, dev, c_down, c_up, c_d1, c_u1, 1, True)
    pieces = (down, up, d1, u1, v4, d2, u2, near, *exchange_wide(d2, u2))
    hid, hid_s, pre, hid_down, hid_up, hid_last, sh_feat = call(
        forward_kernel,
        [
            ((BD, 512, CH), BF),
            ((BD * 512, CH), BF),
            ((BD * 512, CH), F32),
            *halo(1),
            (SHIFTED, BF),
        ],
        scratch_own() + scratch_build(),
        nb,
        dev,
        feat,
        *pieces,
        w_one,
    )
    tied = (c_d2, c_u2, c_near, c_v4), (hid_down, hid_up, hid_last)
    (c_d2, c_u2, c_near, c_v4), (hid_down, hid_up, hid_last) = lax.optimization_barrier(tied)
    d1, u1, v4 = exchange_near(hid_down, hid_up, hid_last)
    c_wide = exchange_wide(c_d2, c_u2)
    pieces = (c_down, c_up, c_d1, c_u1, c_v4, c_d2, c_u2, c_near, *c_wide)
    sh_cot, hid_t, delta_t = call(
        backward_kernel,
        [(SHIFTED, BF), ((CH, BD * 512), BF), ((CH, BD * 512), BF)],
        scratch_own() + scratch_build() + [pltpu.VMEM((BD * 512, CH), BF)],
        nb,
        dev,
        cot,
        *pieces,
        flipped,
        hid_s,
        pre,
    )
    d1, u1, hid_t, delta_t, sh_cot = lax.optimization_barrier((d1, u1, hid_t, delta_t, sh_cot))
    h_far = exchange_far(nb, dev, hid_down, hid_up, d1, u1, 1)[:3]
    keep, send = call(
        gradient_kernel,
        [((27 * CH, CH), F32)] * 2,
        [],
        nb,
        dev,
        hid_t,
        delta_t,
        sh_feat,
        sh_cot,
    )
    voxel_total = lax.axis_size("rep") * lax.axis_size("blocks") * BD * 512
    scale = 1.0 / math.sqrt(voxel_total)

    def second(far):
        return call(
            second_kernel,
            [((BD, 512, CH), BF)],
            scratch_own() + scratch_build() + [pltpu.VMEM(SHIFTED, BF)],
            nb,
            dev,
            hid,
            hid_down,
            hid_up,
            d1,
            u1,
            v4,
            *far,
            *exchange_wide(far[0], far[1]),
            w_two,
        )[0]

    grad_one, grad_two, out = reduce_all(keep, send, core, scale, second, h_far, nb, dev)
    return out[None], grad_one, grad_two


def solution(mesh):
    in_specs = (
        P("rep", "blocks", None, None),
        P(),
        P(),
        P("rep", "blocks", None, None),
        P("rep", "blocks", None),
    )
    out_specs = (P("rep", "blocks", None, None), P(), P())
    return jax.shard_map(slab_step, mesh=mesh, in_specs=in_specs, out_specs=out_specs, check_vma=False)
```

```python
import functools
import math

import jax
import jax.numpy as jnp
from jax import lax
from jax.experimental import pallas as pl
from jax.experimental.pallas import tpu as pltpu
from jax.sharding import PartitionSpec as P


CH = 128
BD = 4
RX, RE, RP = 256, 128, 256
FULL, MID, FAR = RX + RE + 2 * RP, RX + RE, RX
SLOTS = 20

OFFSETS = [
    (dx, dy, dz)
    for dx in (-1, 0, 1)
    for dy in (-1, 0, 1)
    for dz in (-1, 0, 1)
    if (dx, dy, dz) != (0, 0, 0)
]
K_OF = {offset: k for k, offset in enumerate(OFFSETS)}
BF = jnp.bfloat16
F32 = jnp.float32


def pack_field(nb, dev, own, down, up, last, f):
    ox = f * FULL
    oe, oj, ol = ox + RX, ox + RX + RE, ox + RX + RE + RP

    def body(b, carry):
        me = dev * BD + b

        def neighbour(offset):
            return nb[b, K_OF[offset]]

        y_hi, y_lo = neighbour((0, 1, 0)), neighbour((0, -1, 0))
        z_hi, z_lo = neighbour((0, 0, 1)), neighbour((0, 0, -1))
        cases = (
            (down, 0, (y_hi >= 0) & (y_hi < me), (z_hi >= 0) & (z_hi < me)),
            (up, 448, jnp.logical_not(y_lo > me), jnp.logical_not(z_lo > me)),
        )
        edges = jnp.concatenate(
            [own[b, pl.ds(js * 8 + ls, 8, stride=64), :] for js in (0, 7) for ls in (0, 7)], axis=0
        ).astype(BF)
        z_low = own[b, pl.ds(0, 64, stride=8), :]
        z_high = own[b, pl.ds(7, 64, stride=8), :]
        y_low = jnp.concatenate([own[b, i * 64 : i * 64 + 8, :] for i in range(8)], axis=0)
        y_high = jnp.concatenate([own[b, i * 64 + 56 : i * 64 + 64, :] for i in range(8)], axis=0)
        for ref, x_row, take_y, take_z in cases:
            ref[pl.ds(pl.multiple_of(ox + b * 64, 64), 64), :] = own[b, x_row : x_row + 64, :].astype(BF)
            ref[pl.ds(pl.multiple_of(oe + b * 32, 32), 32), :] = edges
            ref[pl.ds(pl.multiple_of(oj + b * 64, 64), 64), :] = jnp.where(take_y, y_high, y_low).astype(BF)
            ref[pl.ds(pl.multiple_of(ol + b * 64, 64), 64), :] = jnp.where(take_z, z_high, z_low).astype(BF)
        return carry

    lax.fori_loop(0, BD, body, 0)
    if last is None:
        return
    first = (dev & 1) == 0

    @pl.when(first)
    def _():
        last[f * FAR : f * FAR + FAR, :] = down[ox : ox + FAR, :]

    @pl.when(jnp.logical_not(first))
    def _():
        last[f * FAR : f * FAR + FAR, :] = up[ox : ox + FAR, :]


def fill_tables(core, pieces, tx, te, tj, tl, fields=1, f=0):
    own_down, own_up, d1, u1, v4, d2, u2, near, wide_d, wide_u = pieces
    turn = 2 * core
    full, two = f * FULL, f * (MID + FAR)
    plan = [
        (own_down, full, 10, 4),
        (own_up, full, 9, 4),
        (d1, full, 12, 4),
        (u1, full, 7, 4),
        (d2, two, 14, 2),
        (u2, two, 5, 2),
        (d2, two + MID, 16, 1),
        (u2, two + MID, 3, 1),
        (v4, f * FAR, 2 + 15 * core, 1),
        (near, full, 11 - 3 * core, 4),
        (near, full + fields * FULL, 13 - turn, 4),
        (near, full + 2 * fields * FULL, 8 - turn, 4),
        (wide_d, two, 15 - turn, 2),
        (wide_u, two, 6 - turn, 2),
        (wide_d, two + MID, 17 - turn, 1),
        (wide_u, two + MID, 4 - turn, 1),
    ]
    for ref, row, slot, kind in plan:
        tx[slot] = ref[row : row + RX, :].astype(F32).reshape(BD, 64, CH)
        if kind >= 2:
            row += RX
            te[slot] = ref[row : row + RE, :].astype(F32).reshape(BD, 32, CH)
        if kind >= 4:
            row += RE
            tj[slot] = ref[row : row + RP, :].astype(F32).reshape(BD, 64, CH)
            row += RP
            tl[slot] = ref[row : row + RP, :].astype(F32).reshape(BD, 64, CH)


def build_shifted(nb, dev, own, tx, te, tj, tl, cf, lf, rf, sh):
    def block(b, carry):
        me = dev * BD + b

        def source(offset):
            n = nb[b, K_OF[offset]]
            gap = lax.shift_right_logical(jnp.maximum(n, 0), 2) - dev
            slot = jnp.clip(jnp.where(n > me, 10 + gap, 9 + gap), 0, SLOTS - 1)
            return n >= 0, slot, jnp.maximum(n, 0) & 3

        def keep(valid, rows):
            return jnp.where(valid, rows, jnp.zeros_like(rows))

        for i in range(8):
            cf[b, pl.ds((i + 1) * 80 + 8, 64), :] = own[b, pl.ds(i * 64, 64), :]
        for dy, line in ((-1, 0), (1, 9)):
            valid, slot, loc = source((0, dy, 0))
            for i in range(8):
                rows = tj[slot, loc, pl.ds(i * 8, 8), :]
                cf[b, pl.ds((i + 1) * 80 + line * 8, 8), :] = keep(valid, rows)
        for dx, plane in ((-1, 0), (1, 9)):
            valid, slot, loc = source((dx, 0, 0))
            cf[b, pl.ds(plane * 80 + 8, 64), :] = keep(valid, tx[slot, loc])
            for dy, line, j in ((-1, 0, 7), (1, 9, 0)):
                valid, slot, loc = source((dx, dy, 0))
                rows = tx[slot, loc, pl.ds(j * 8, 8), :]
                cf[b, pl.ds(plane * 80 + line * 8, 8), :] = keep(valid, rows)
        for plane in range(10):
            lines = cf[b, pl.ds(plane * 80, 80), :].reshape(10, 8, CH)
            lf[b, pl.ds(plane * 80, 80), :] = pltpu.roll(lines, 1, 1).reshape(80, CH)
            rf[b, pl.ds(plane * 80, 80), :] = pltpu.roll(lines, 7, 1).reshape(80, CH)
        for dz, ref, cell, l in ((-1, lf, 0, 7), (1, rf, 7, 0)):
            valid, slot, loc = source((0, 0, dz))
            for i in range(8):
                rows = tl[slot, loc, pl.ds(i * 8, 8), :]
                ref[b, pl.ds((i + 1) * 80 + 8 + cell, 8, stride=8), :] = keep(valid, rows)
            for dy, line, j in ((-1, 0, 7), (1, 9, 0)):
                valid, slot, loc = source((0, dy, dz))
                edge = (2 * (j // 7) + l // 7) * 8
                rows = te[slot, loc, pl.ds(edge, 8), :]
                ref[b, pl.ds(80 + line * 8 + cell, 8, stride=80), :] = keep(valid, rows)
            for dx, plane in ((-1, 0), (1, 9)):
                valid, slot, loc = source((dx, 0, dz))
                rows = tx[slot, loc, pl.ds(l, 8, stride=8), :]
                ref[b, pl.ds(plane * 80 + 8 + cell, 8, stride=8), :] = keep(valid, rows)
                for dy, line, j in ((-1, 0, 7), (1, 9, 0)):
                    valid, slot, loc = source((dx, dy, dz))
                    rows = tx[slot, loc, pl.ds(j * 8 + l, 1), :]
                    ref[b, pl.ds(plane * 80 + line * 8 + cell, 1), :] = keep(valid, rows)
        return carry

    lax.fori_loop(0, BD, block, 0)

    def join(plane, carry):
        row = pl.multiple_of(plane * 80, 80)
        for pair in range(2):
            for c, ref in ((0, lf), (1, cf), (2, rf)):
                halves = [ref[2 * pair + h, pl.ds(row, 80), :].reshape(10, 8, CH) for h in (0, 1)]
                sh[c, pair, plane] = jnp.concatenate(halves, axis=1).astype(BF)
        return carry

    lax.fori_loop(0, 10, join, 0)


def slabs(sh, pair, first, count, taps):
    return jnp.concatenate(
        [
            sh[c, pair, pl.ds(first + a, count), b : b + 8].reshape(count * 128, CH)
            for a, b, c in taps
        ],
        axis=1,
    )


TAPS = [(a, b, c) for a in range(3) for b in range(3) for c in range(3)]
CHUNK = 4


def conv(sh, weight, emit):
    def body(step, carry):
        pair = step // (8 // CHUNK)
        first = (step % (8 // CHUNK)) * CHUNK
        rows = jnp.dot(slabs(sh, pair, first, CHUNK, TAPS), weight[...], preferred_element_type=F32)
        emit(pair, first, rows)
        return carry

    lax.fori_loop(0, 2 * (8 // CHUNK), body, 0)


def split_blocks(pair, first, rows, store):
    lines = rows.reshape(CHUNK * 8, 16, CH)
    for h in (0, 1):
        part = lines[:, 8 * h : 8 * h + 8].reshape(CHUNK * 64, CH)
        store(2 * pair + h, pl.multiple_of(first * 64, 64), part)


def load_own(ref, own):
    for b in range(BD):
        own[b] = ref[b].astype(F32)


def pack_kernel(nb, dev, field, down, up, own):
    load_own(field, own)
    pack_field(nb, dev[0], own, down, up, None, 0)


def flip_kernel(nb, dev, weight, out):
    for t in range(27):
        out[t * CH : t * CH + CH, :] = weight[(26 - t) * CH : (27 - t) * CH, :].T


def forward_kernel(nb, dev, feat, *refs):
    pieces, weight = refs[:10], refs[10]
    hid, hid_s, pre, down, up, last, sh, own, tx, te, tj, tl, cf, lf, rf = refs[11:]
    load_own(feat, own)
    fill_tables(dev[0] & 1, pieces, tx, te, tj, tl)
    build_shifted(nb, dev[0], own, tx, te, tj, tl, cf, lf, rf, sh)

    def emit(pair, first, rows):
        at = pl.ds(pl.multiple_of(pair * 1024 + first * 128, 128), CHUNK * 128)
        pre[at, :] = rows
        act = (rows / (1.0 + jnp.exp(-rows))).astype(BF)
        hid_s[at, :] = act

        def store(b, row, part):
            own[b, pl.ds(row, CHUNK * 64), :] = part
            hid[b, pl.ds(row, CHUNK * 64), :] = part.astype(BF)

        split_blocks(pair, first, act.astype(F32), store)

    conv(sh, weight, emit)
    pack_field(nb, dev[0], own, down, up, last, 0)


def backward_kernel(nb, dev, cot, *refs):
    pieces, weight, hid_s, pre = refs[:10], refs[10], refs[11], refs[12]
    sh, hid_t, delta_t, own, tx, te, tj, tl, cf, lf, rf, delta = refs[13:]
    load_own(cot, own)
    fill_tables(dev[0] & 1, pieces, tx, te, tj, tl)
    build_shifted(nb, dev[0], own, tx, te, tj, tl, cf, lf, rf, sh)

    def emit(pair, first, rows):
        at = pl.ds(pl.multiple_of(pair * 1024 + first * 128, 128), CHUNK * 128)
        v = pre[at, :]
        sig = 1.0 / (1.0 + jnp.exp(-v))
        delta[at, :] = (rows * (sig * (1.0 + v * (1.0 - sig)))).astype(BF)

    conv(sh, weight, emit)
    for pair in range(2):
        at = slice(pair * 1024, pair * 1024 + 1024)
        hid_t[:, at] = hid_s[at, :].T
        delta_t[:, at] = delta[at, :].T


def gradient_kernel(nb, dev, hid_t, delta_t, sh_feat, sh, keep, send):
    def body(a, carry):
        def product(left, ref):
            right = jnp.concatenate(
                [
                    jnp.concatenate(
                        [ref[c, pair, pl.ds(a, 8), b : b + 8].reshape(1024, CH) for b in range(3) for c in range(3)],
                        axis=1,
                    )
                    for pair in range(2)
                ],
                axis=0,
            )
            return jnp.dot(left[...], right, preferred_element_type=F32)

        def write(first, second):
            one = product(delta_t, sh_feat)
            for t in range(9):
                row = pl.multiple_of((a * 9 + t) * CH, CH)
                first[pl.ds(row, CH), :] = one[:, t * CH : t * CH + CH].T
            two = product(hid_t, sh)
            for t in range(9):
                row = pl.multiple_of((26 - a * 9 - t) * CH, CH)
                second[pl.ds(row, CH), :] = two[:, t * CH : t * CH + CH]

        @pl.when((dev[0] & 1) == 0)
        def _():
            write(keep, send)

        @pl.when((dev[0] & 1) == 1)
        def _():
            write(send, keep)

        return carry

    lax.fori_loop(0, 3, body, 0)


def second_kernel(nb, dev, hid, *refs):
    pieces, weight, out = refs[:10], refs[10], refs[11]
    own, tx, te, tj, tl, cf, lf, rf, sh = refs[12:]
    load_own(hid, own)
    fill_tables(dev[0] & 1, pieces, tx, te, tj, tl)
    build_shifted(nb, dev[0], own, tx, te, tj, tl, cf, lf, rf, sh)

    def emit(pair, first, rows):
        def store(b, row, part):
            out[b, pl.ds(row, CHUNK * 64), :] = part.astype(BF)

        split_blocks(pair, first, rows, store)

    conv(sh, weight, emit)


def scratch_own():
    return [pltpu.VMEM((BD, 512, CH), F32)]


def scratch_build():
    return [
        pltpu.VMEM((SLOTS, BD, 64, CH), F32),
        pltpu.VMEM((SLOTS, BD, 32, CH), F32),
        pltpu.VMEM((SLOTS, BD, 64, CH), F32),
        pltpu.VMEM((SLOTS, BD, 64, CH), F32),
    ] + [pltpu.VMEM((BD, 800, CH), F32)] * 3


SHIFTED = (3, 2, 10, 10, 16, CH)
LIMIT = 26


def call(kernel, outs, scratch, nb, dev, *arrays, limit=LIMIT):
    smem = pl.BlockSpec(memory_space=pltpu.SMEM)
    vmem = pl.BlockSpec(memory_space=pltpu.VMEM)
    return pl.pallas_call(
        kernel,
        out_shape=[jax.ShapeDtypeStruct(shape, dtype) for shape, dtype in outs],
        in_specs=[smem, smem] + [vmem] * len(arrays),
        out_specs=[vmem] * len(outs),
        scratch_shapes=scratch,
        compiler_params=pltpu.CompilerParams(vmem_limit_bytes=limit << 20),
    )(nb, dev, *arrays)


def hop(x, shift):
    size = lax.axis_size("blocks")
    return lax.ppermute(x, "blocks", [(i, (i + shift(i)) % size) for i in range(size)])


def swap(x):
    return hop(x, lambda i: 1 - 2 * (i % 2))


def exchange_near(down, up, last):
    d1, u1 = hop(down, lambda i: -2), hop(up, lambda i: 2)
    if last is None:
        return d1, u1, None
    return d1, u1, hop(last, lambda i: -7 if i % 2 == 0 else 7)


def forward_planes(fields, nb, dev, down, up, d1, u1, far_down, far_up, near, *last):
    full = fields * FULL
    for own, got, out in ((down, d1, far_down), (up, u1, far_up)):
        for f in range(fields):
            at, row = f * (MID + FAR), f * FULL
            out[at : at + MID, :] = own[row : row + MID, :]
            out[at + MID : at + MID + FAR, :] = got[row : row + FAR, :]
    near[full : 2 * full, :] = d1[...]
    near[2 * full : 3 * full, :] = u1[...]
    first = (dev[0] & 1) == 0

    @pl.when(first)
    def _():
        near[0:full, :] = up[...]
        for ref in last:
            ref[...] = d1[0:FAR, :]

    @pl.when(jnp.logical_not(first))
    def _():
        near[0:full, :] = down[...]
        for ref in last:
            ref[...] = u1[0:FAR, :]


def exchange_far(nb, dev, down, up, d1, u1, fields, diagonal=False):
    outs = [((fields * (MID + FAR), CH), BF)] * 2 + [((3 * fields * FULL, CH), BF)]
    outs += [((FAR, CH), BF)] * diagonal
    kernel = functools.partial(forward_planes, fields)
    far_down, far_up, near, *last = call(kernel, outs, [], nb, dev, down, up, d1, u1, limit=8)
    v4 = hop(last[0], lambda i: -5 if i % 2 == 0 else 5) if diagonal else None
    d2 = hop(far_down, lambda i: -4)
    u2 = hop(far_up, lambda i: 4)
    return d2, u2, swap(near), v4


def exchange_wide(d2, u2):
    return swap(d2), swap(u2)


def sum_kernel(scale, nb, dev, parts, out):
    total = parts[0].astype(F32)
    for k in range(1, parts.shape[0]):
        total = total + parts[k].astype(F32)
    if scale is not None:
        total = total * scale
    total = total.astype(BF)
    for k in range(out.shape[0]):
        out[k] = total


def sum_and_spread(parts, copies, scale, nb, dev):
    kernel = functools.partial(sum_kernel, scale)
    return call(kernel, [((copies, *parts.shape[1:]), BF)], [], nb, dev, parts, limit=8)[0]


def all_to_all(x, axes, groups):
    return lax.all_to_all(x, axes, 0, 0, axis_index_groups=groups, tiled=True)


def reduce_all(keep, send, core, scale, work, given, nb, dev):
    size, reps = lax.axis_size("blocks"), lax.axis_size("rep")
    length = 8
    width = size // (2 * length)
    planes = [
        [(2 * length * x + 2 * z + c) * reps + r for x in range(width) for r in range(reps)]
        for z in range(length)
        for c in range(2)
    ]
    columns = [
        [2 * length * x + 2 * z + c for z in range(length)] for x in range(width) for c in range(2)
    ]
    both = ("blocks", "rep")
    count = width * reps
    rows = keep.shape[0] // count
    mine = keep + swap(send)
    mine, given = lax.optimization_barrier((mine.astype(BF), given))
    given = (*given, *exchange_wide(given[0], given[1]))
    part = all_to_all(mine.reshape(count, rows, CH), both, planes)
    part = sum_and_spread(part, length, None, nb, dev)
    part, given = lax.optimization_barrier((part, given))
    done = work(given)
    part = sum_and_spread(all_to_all(part, "blocks", columns), count, scale, nb, dev)
    part, done = lax.optimization_barrier((part, done))
    mine = all_to_all(part, both, planes).reshape(keep.shape)
    theirs = swap(mine)
    shape = (keep.shape[0] // CH, CH, CH)
    one = jnp.where(core == 0, mine, theirs).astype(F32).reshape(shape)
    two = jnp.where(core == 0, theirs, mine).astype(F32).reshape(shape)
    return one, two, done


def slab_step(features, weight_one, weight_two, cotangent, neighbours):
    feat, cot, nb = features[0], cotangent[0], neighbours[0]
    index = lax.axis_index("blocks")
    core = index % 2
    dev = index.astype(jnp.int32).reshape(1)
    w_one = weight_one.reshape(27 * CH, CH)
    w_two = weight_two.reshape(27 * CH, CH)

    def halo(fields):
        return [((fields * FULL, CH), BF)] * 2 + [((fields * FAR, CH), BF)]

    down, up = call(pack_kernel, halo(1)[:2], scratch_own(), nb, dev, feat)
    d1, u1, _ = exchange_near(down, up, None)
    c_down, c_up = call(pack_kernel, halo(1)[:2], scratch_own(), nb, dev, cot)
    c_d1, c_u1, _ = exchange_near(c_down, c_up, None)
    (flipped,) = call(flip_kernel, [((27 * CH, CH), BF)], [], nb, dev, w_two, limit=8)
    d1, u1, flipped = lax.optimization_barrier((d1, u1, flipped))
    d2, u2, near, v4 = exchange_far(nb, dev, down, up, d1, u1, 1, True)
    c_d2, c_u2, c_near, c_v4 = exchange_far(nb, dev, c_down, c_up, c_d1, c_u1, 1, True)
    pieces = (down, up, d1, u1, v4, d2, u2, near, *exchange_wide(d2, u2))
    hid, hid_s, pre, hid_down, hid_up, hid_last, sh_feat = call(
        forward_kernel,
        [
            ((BD, 512, CH), BF),
            ((BD * 512, CH), BF),
            ((BD * 512, CH), F32),
            *halo(1),
            (SHIFTED, BF),
        ],
        scratch_own() + scratch_build(),
        nb,
        dev,
        feat,
        *pieces,
        w_one,
    )
    tied = (c_d2, c_u2, c_near, c_v4), (hid_down, hid_up, hid_last)
    (c_d2, c_u2, c_near, c_v4), (hid_down, hid_up, hid_last) = lax.optimization_barrier(tied)
    d1, u1, v4 = exchange_near(hid_down, hid_up, hid_last)
    c_wide = exchange_wide(c_d2, c_u2)
    pieces = (c_down, c_up, c_d1, c_u1, c_v4, c_d2, c_u2, c_near, *c_wide)
    sh_cot, hid_t, delta_t = call(
        backward_kernel,
        [(SHIFTED, BF), ((CH, BD * 512), BF), ((CH, BD * 512), BF)],
        scratch_own() + scratch_build() + [pltpu.VMEM((BD * 512, CH), BF)],
        nb,
        dev,
        cot,
        *pieces,
        flipped,
        hid_s,
        pre,
    )
    d1, u1, hid_t, delta_t, sh_cot = lax.optimization_barrier((d1, u1, hid_t, delta_t, sh_cot))
    h_far = exchange_far(nb, dev, hid_down, hid_up, d1, u1, 1)[:3]
    keep, send = call(
        gradient_kernel,
        [((27 * CH, CH), F32)] * 2,
        [],
        nb,
        dev,
        hid_t,
        delta_t,
        sh_feat,
        sh_cot,
    )
    voxel_total = lax.axis_size("rep") * lax.axis_size("blocks") * BD * 512
    scale = 1.0 / math.sqrt(voxel_total)

    def second(far):
        return call(
            second_kernel,
            [((BD, 512, CH), BF)],
            scratch_own() + scratch_build() + [pltpu.VMEM(SHIFTED, BF)],
            nb,
            dev,
            hid,
            hid_down,
            hid_up,
            d1,
            u1,
            v4,
            *far,
            w_two,
        )[0]

    grad_one, grad_two, out = reduce_all(keep, send, core, scale, second, h_far, nb, dev)
    return out[None], grad_one, grad_two


def solution(mesh):
    in_specs = (
        P("rep", "blocks", None, None),
        P(),
        P(),
        P("rep", "blocks", None, None),
        P("rep", "blocks", None),
    )
    out_specs = (P("rep", "blocks", None, None), P(), P())
    return jax.shard_map(slab_step, mesh=mesh, in_specs=in_specs, out_specs=out_specs, check_vma=False)
```
